32 devices in a mesh: layer: 2 (over core), tok: 16 (over z, y, x).
Axes of the slice: x: 2, y: 2, z: 4, core: 2. Of those that a mesh axis runs over, the one named last changes fastest.
Arguments:
- train_act: bfloat16 [4, 32768, 256], P('layer', 'tok'), may hold values from -0.75 to 0.75
- train_grad: bfloat16 [4, 32768, 256], P('layer', 'tok'), may hold values from -0.75 to 0.75
- test_act: bfloat16 [4, 2048, 256], P('layer', 'tok'), may hold values from -0.75 to 0.75
- test_grad: bfloat16 [4, 2048, 256], P('layer', 'tok'), may hold values from -0.75 to 0.75
- segment_ids: int32 [2048], replicated, may hold values from 0 to 127, as said below
Outputs:
- scores: float32 [128, 32768], P('layer', 'tok')
The draws below stay inside these ranges and needn't reach their ends.
Inputs may be any that keep to these rules, and one draw needn't show every extreme that they name: `segment_ids`: each of the 128 queries has exactly 16 test tokens, placed anywhere among the 2048.
All inputs are finite; a program needn't handle non-finite values.
Results may differ from the reference program's by a relative error of at most 0.0029.
Values may be sent and summed in bfloat16 or wider, within the bound.
A program may use at most 128 MiB of HBM per device.

```python
import jax
import jax.numpy as jnp
from jax import lax

P_SIZE = 256
Q = 128
QTOK = 16
S = 2048
L = 4
TOKENS = 32768


def draw_segment_ids(key, part):
    order = jax.random.permutation(jax.random.fold_in(key, 7), S)
    return (order // QTOK).astype(jnp.int32)


def steps_of(own_key, dims, cuts, low, top_value):
    def one(position, blocks):
        heights = jax.random.uniform(jax.random.fold_in(jax.random.fold_in(own_key, 6), position), (blocks,), jnp.float32, low / len(cuts), top_value / len(cuts))
        return jnp.repeat(jnp.exp(heights), dims[position] // blocks).reshape((-1,) + (1,) * (len(dims) - position - 1))

    level = one(*cuts[0])
    for cut in cuts[1:]:
        level = level * one(*cut)
    return level


def bell_draw(key, shape, deviation, reach, pieces=(), kind=jnp.bfloat16):
    values = jax.random.normal(key, shape, jnp.float32) * deviation
    if len(pieces) > 0:
        values = steps_of(key, shape, pieces, -0.22, 0.18) * values
    return jnp.clip(values, min=-reach, max=reach).astype(kind)


def setup_inputs(seed: int = 0) -> dict:
    keys = jax.random.split(jax.random.key(seed), 6)
    return {
        "train_act": bell_draw(keys[0], (L, TOKENS, P_SIZE), 0.125, 0.75, ((0, 2), (1, 16))),
        "train_grad": bell_draw(keys[1], (L, TOKENS, P_SIZE), 0.125, 0.75, ((0, 2), (1, 16))),
        "test_act": bell_draw(keys[2], (L, S, P_SIZE), 0.125, 0.75, ((0, 2), (1, 16))),
        "test_grad": bell_draw(keys[3], (L, S, P_SIZE), 0.125, 0.75, ((0, 2), (1, 16))),
        "segment_ids": draw_segment_ids(jax.random.fold_in(keys[5], 71), 0),
    }


def reference(train_act, train_grad, test_act, test_grad, segment_ids):
    labels = jnp.arange(Q, dtype=jnp.int32)[:, None]
    select = (segment_ids[None, :] == labels).astype(jnp.bfloat16)

    def one_layer(running, tensors):
        act_train, grad_train, act_test, grad_test = tensors
        act_gram = jnp.einsum("sp,tp->st", act_test.astype(jnp.float32), act_train.astype(jnp.float32))
        grad_gram = jnp.einsum("sp,tp->st", grad_test.astype(jnp.float32), grad_train.astype(jnp.float32))
        product = (act_gram * grad_gram).astype(jnp.bfloat16)
        return running + jnp.dot(select, product, preferred_element_type=jnp.float32), None

    initial = jnp.zeros((Q, train_act.shape[1]), jnp.float32)
    scores, _ = lax.scan(one_layer, initial, (train_act, train_grad, test_act, test_grad))
    return scores
```

```python
import functools
import heapq
import math

import jax
import jax.numpy as jnp
from jax import lax
from jax.experimental import pallas as pl
from jax.experimental.pallas import tpu as pltpu
from jax.sharding import PartitionSpec as P

Q = 128
MESH = pl.DeviceIdType.MESH
OWN, XSIDE, YSIDE, DIAG = range(4)
ACT, GRAD = range(2)

CHUNK_TIME = 1.4
HOP_TIME = 1.7
POLL_TIME = 0.5
LOAD_TIME = 3.0
UNIT_TIME = 1.0


def route_blocks(line, layers):
    reach = (2 + line) // 3
    even = line % 2 == 0
    free, events, log = {}, [], [[] for _ in range(line)]

    def flipped(at):
        return even and 2 * at > line - 1

    def send(time, at, route, chunk):
        start = max(free.get((at, route), 0.0), time)
        free[at, route] = start + CHUNK_TIME
        there = at + {"x": 0, "y": 0, "up": 1, "down": -1}[route]
        column, plane, which, layer = chunk
        seen = line - 1 - plane if flipped(there) else plane
        role = line - 1 - there if flipped(there) else there
        key = (round(start + CHUNK_TIME + HOP_TIME, 3), role, seen, column, layer, which, there)
        heapq.heappush(events, (key, chunk))

    def passes(at, chunk):
        column, plane, which, layer = chunk
        along = []
        if plane <= at < line - 1:
            along.append(("up", at + 1))
        if plane >= at > 0:
            along.append(("down", at - 1))
        if flipped(at):
            along.reverse()
        distance = abs(plane - at)
        far = distance > reach
        out = []
        if column == OWN:
            out += [(route, chunk) for route, _ in along]
            if plane != at:
                out.append(("y", (YSIDE, plane, which, layer)))
                late = far and layer == layers - 1
                if which == GRAD or not late:
                    out.append(("x", (XSIDE, plane, which, layer)))
                if which == GRAD and late:
                    out.append(("x", (XSIDE, plane, ACT, layer)))
        if column == DIAG:
            out += [(route, chunk) for route, to in along if abs(plane - to) <= reach]
        if far or distance == 0:
            if column == YSIDE and which == ACT:
                out.append(("x", (DIAG, plane, which, layer)))
            if column == XSIDE and which == GRAD:
                out.append(("y", (DIAG, plane, which, layer)))
        return out

    first = []
    for at in range(line):
        mine = []
        for i in range(2 * layers):
            mine += passes(at, (OWN, at, i % 2, i // 2))
            mine.append(("x", (XSIDE, at, 1 - i // layers, i % layers)))
            mine.append(("y", (YSIDE, at, i // layers, i % layers)))
        for route, chunk in mine:
            send(0.0, at, route, chunk)
        first.append(mine)
    while events:
        (time, *_, at), chunk = heapq.heappop(events)
        out = passes(at, chunk)
        for route, sent in out:
            send(time + POLL_TIME, at, route, sent)
        log[at].append((time, chunk, out))
    return first, log


def plan_steps(at, line, layers, log):
    ready = {(OWN, at, layer): 0.0 for layer in range(layers)}
    for time, (column, plane, _, layer), _ in log:
        ready[column, plane, layer] = max(time, ready.get((column, plane, layer), 0.0))
    blocks = sorted(
        {key[:2] for key in ready}, key=lambda b: [ready[(*b, l)] for l in range(layers)][::-1]
    )
    units = []
    for one, two in zip(blocks[::2], blocks[1::2]):
        for layer in range(layers):
            units.append((max(ready[(*one, layer)], ready[(*two, layer)]), one, two, layer))
    units.sort(key=lambda unit: unit[0])
    steps, now, i = [], LOAD_TIME, 0
    for k, (time, one, two, layer) in enumerate(units):
        now = max(now, time)
        moves = []
        while i < len(log) and (log[i][0] <= now or k == len(units) - 1):
            moves.append(log[i][1:])
            i += 1
        steps.append((moves, one, two, layer))
        now += UNIT_TIME
    return steps


def branch(value, low, high, leaf):
    if high - low == 1:
        leaf(low)
        return
    middle = (low + high) // 2
    pl.when(value < middle)(lambda: branch(value, low, middle, leaf))
    pl.when(value >= middle)(lambda: branch(value, middle, high, leaf))


def pick(index, values):
    result = jnp.int32(values[-1])
    for i, value in enumerate(values[:-1]):
        result = jnp.where(index == i, jnp.int32(value), result)
    return result


def kernel(
    layers,
    line,
    train_a,
    train_g,
    test_a,
    test_g,
    ids_ref,
    out_ref,
    ta,
    tg,
    buf,
    acc,
    xbuf,
    train_sem,
    own_sem,
    recv_sem,
    send_sem,
    xs_sem,
    xr_sem,
):
    me = lax.axis_index("tok")
    core = lax.axis_index("layer")
    z = me // 4
    y = (me // 2) % 2
    x = me % 2
    columns = (
        y * 2 + x,
        y * 2 + (1 - x),
        (1 - y) * 2 + x,
        (1 - y) * 2 + (1 - x),
    )
    layer_count, train_rows, _ = ta.shape
    _, rows, width = buf.shape
    q_block = Q // layers
    has_up = z < line - 1
    has_down = z > 0

    roles = line // 2 if line % 2 == 0 else line
    flip = (z >= roles).astype(jnp.int32)
    role = jnp.where(flip == 1, line - 1 - z, z)
    sign = 1 - 2 * flip
    partner = {
        "x": z * 4 + columns[XSIDE],
        "y": z * 4 + columns[YSIDE],
        "up": me + 4 * sign,
        "down": me - 4 * sign,
    }
    routes = tuple(partner)
    across = {
        "x": (XSIDE, OWN, DIAG, YSIDE),
        "y": (YSIDE, DIAG, OWN, XSIDE),
        "up": (OWN, XSIDE, YSIDE, DIAG),
        "down": (OWN, XSIDE, YSIDE, DIAG),
    }

    def place(column, plane):
        return jnp.where(flip == 1, line - 1 - plane, plane) * 4 + columns[column]

    def slot(column, plane, which, layer):
        return (place(column, plane) * layer_count + layer) * 2 + which

    for which, (src, dst) in enumerate(((train_a, ta), (train_g, tg))):
        pltpu.make_async_copy(src, dst, train_sem.at[which]).start()

    def own_copy(which, layer):
        src = (test_a, test_g)[which]
        return pltpu.make_async_copy(
            src.at[layer],
            buf.at[(me * layer_count + layer) * 2 + which],
            own_sem.at[which, layer],
        )

    for which in range(2):
        for layer in range(layer_count):
            own_copy(which, layer).start()

    barrier = pltpu.get_barrier_semaphore()

    def greet(where):
        pl.semaphore_signal(barrier, inc=1, device_id=where, device_id_type=MESH)

    greet({"tok": partner["x"]})
    greet({"tok": partner["y"]})
    pl.when(has_up)(lambda: greet({"tok": me + 4}))
    pl.when(has_down)(lambda: greet({"tok": me - 4}))
    for step in range(1, layers):
        greet({"layer": lax.rem(core + step, layers)})
    ends = jnp.where(has_up, 1, 0) + jnp.where(has_down, 1, 0)
    pl.semaphore_wait(barrier, layers + 1 + ends)

    def copy(route, chunk, src=None):
        column, plane, which, layer = chunk
        here = slot(across[route][column], plane, which, layer)
        return pltpu.make_async_remote_copy(
            src_ref=buf.at[here] if src is None else src,
            dst_ref=buf.at[here],
            send_sem=send_sem.at[routes.index(route)],
            recv_sem=recv_sem.at[here],
            device_id={"tok": partner[route]},
            device_id_type=MESH,
        )

    def arrived(chunk):
        here = slot(*chunk)
        pltpu.make_async_remote_copy(
            src_ref=buf.at[here],
            dst_ref=buf.at[here],
            send_sem=send_sem.at[0],
            recv_sem=recv_sem.at[here],
            device_id={"tok": partner["x"]},
            device_id_type=MESH,
        ).wait_recv()

    first, log = route_blocks(line, layer_count)
    steps = [plan_steps(at, line, layer_count, log[at]) for at in range(roles)]
    count = len(steps[0])

    def send_own(at):
        for route, chunk in first[at]:
            copy(route, chunk, (test_a, test_g)[chunk[2]].at[chunk[3]]).start()

    branch(role, 0, roles, send_own)

    acc[...] = jnp.zeros_like(acc)
    _, tiles, _, tile = xbuf.shape
    labels = lax.broadcasted_iota(jnp.int32, (Q, rows), 0)
    nt = (((1,), (1,)), ((), ()))

    def exchange(step, j):
        to = lax.rem(core + step, layers)
        theirs = pl.ds(pl.multiple_of(to * q_block, q_block), q_block)
        return pltpu.make_async_remote_copy(
            src_ref=acc.at[theirs, pl.ds(pl.multiple_of(j * tile, tile), tile)],
            dst_ref=xbuf.at[step - 1, j],
            send_sem=xs_sem.at[step - 1, j],
            recv_sem=xr_sem.at[step - 1, j],
            device_id={"layer": to},
            device_id_type=MESH,
        )

    for which in range(2):
        for layer in range(layer_count):
            own_copy(which, layer).wait()
    for which, (src, dst) in enumerate(((train_a, ta), (train_g, tg))):
        pltpu.make_async_copy(src, dst, train_sem.at[which]).wait()

    def relay(k, at):
        for chunk, out in steps[at][k][0]:
            arrived(chunk)
            for route, sent in out:
                copy(route, sent).start()

    base = line * 4
    packed = [
        (
            ((one[1] * 4 + one[0]) * base + two[1] * 4 + two[0]) * layer_count + layer
        )
        for at in range(roles)
        for _, one, two, layer in steps[at]
    ]

    def position(code):
        plane, column = code // 4, code % 4
        plane = jnp.where(flip == 1, line - 1 - plane, plane)
        return plane * 4 + pick(column, columns)

    def step(k, carry):
        branch(k, 0, count, lambda k0: branch(role, 0, roles, functools.partial(relay, k0)))
        code = pick(role * count + k, packed)
        layer = code % layer_count
        one = position(code // layer_count // base)
        two = position((code // layer_count) % base)
        select = jnp.concatenate(
            [
                jnp.where(ids_ref[b] == labels, 1.0, 0.0).astype(jnp.bfloat16)
                for b in (one, two)
            ],
            axis=1,
        )

        def held(which):
            return jnp.concatenate(
                [buf[(b * layer_count + layer) * 2 + which] for b in (one, two)], axis=0
            )

        def one_tile(j, carry):
            at = pl.ds(pl.multiple_of(j * tile, tile), tile)
            a_gram = lax.dot_general(
                held(ACT), ta[layer, at, :], nt, preferred_element_type=jnp.float32
            )
            g_gram = lax.dot_general(
                held(GRAD), tg[layer, at, :], nt, preferred_element_type=jnp.float32
            )
            product = (a_gram * g_gram).astype(jnp.bfloat16)
            acc[:, at] += jnp.dot(select, product, preferred_element_type=jnp.float32)

            @pl.when(k == count - 1)
            def _():
                for step in range(1, layers):
                    exchange(step, j).start()

            return carry

        lax.fori_loop(0, tiles, one_tile, 0)
        return carry

    lax.fori_loop(0, count, step, 0)

    def drain(at):
        sent = list(first[at])
        for moves, *_ in steps[at]:
            for _, out in moves:
                sent += out
        for i, route in enumerate(routes):
            total = sum(r == route for r, _ in sent)
            if total > 0:
                all_of_them = buf.at[pl.ds(0, total)]
                pltpu.make_async_remote_copy(
                    src_ref=all_of_them,
                    dst_ref=all_of_them,
                    send_sem=send_sem.at[i],
                    recv_sem=recv_sem.at[0],
                    device_id={"tok": partner["x"]},
                    device_id_type=MESH,
                ).wait_send()

    branch(role, 0, roles, drain)

    mine = pl.ds(pl.multiple_of(core * q_block, q_block), q_block)
    for j in range(tiles):
        at = pl.ds(j * tile, tile)
        for step in range(1, layers):
            exchange(step, j).wait_recv()
        result = acc[mine, at]
        for step in range(1, layers):
            result = result + xbuf[step - 1, j]
        out_ref[:, at] = result
    for j in range(tiles):
        for step in range(1, layers):
            exchange(step, j).wait_send()


def on_device(layers, toks, train_act, train_grad, test_act, test_grad, segment_ids):
    layer_count, train_rows, width = train_act.shape
    rows = test_act.shape[1]
    line = toks // 4
    tile = math.gcd(train_rows, 1024)
    tiles = train_rows // tile
    q_block = Q // layers
    ids = segment_ids.reshape(toks, 1, rows)
    dma = pltpu.SemaphoreType.DMA
    anywhere = pl.BlockSpec(memory_space=pl.ANY)
    return pl.pallas_call(
        functools.partial(kernel, layers, line),
        out_shape=jax.ShapeDtypeStruct((q_block, train_rows), jnp.float32),
        in_specs=[anywhere] * 4 + [pl.BlockSpec(memory_space=pltpu.VMEM)],
        out_specs=pl.BlockSpec(memory_space=pltpu.VMEM),
        scratch_shapes=[
            pltpu.VMEM((layer_count, train_rows, width), jnp.bfloat16),
            pltpu.VMEM((layer_count, train_rows, width), jnp.bfloat16),
            pltpu.VMEM((toks * layer_count * 2, rows, width), jnp.bfloat16),
            pltpu.VMEM((Q, train_rows), jnp.float32),
            pltpu.VMEM((layers - 1, tiles, q_block, tile), jnp.float32),
            dma((2,)),
            dma((2, layer_count)),
            dma((toks * layer_count * 2,)),
            dma((4,)),
            dma((layers - 1, tiles)),
            dma((layers - 1, tiles)),
        ],
        compiler_params=pltpu.CompilerParams(
            collective_id=0, has_side_effects=True, vmem_limit_bytes=63 * 1024 * 1024
        ),
    )(train_act, train_grad, test_act, test_grad, ids)


def solution(mesh):
    placed = (
        P("layer", "tok", None),
        P("layer", "tok", None),
        P("layer", "tok", None),
        P("layer", "tok", None),
        P(),
    )
    body = functools.partial(on_device, mesh.shape["layer"], mesh.shape["tok"])
    return jax.shard_map(
        body, mesh=mesh, in_specs=placed, out_specs=P("layer", "tok"), check_vma=False
    )
```

```python
import functools
import heapq
import math

import jax
import jax.numpy as jnp
from jax import lax
from jax.experimental import pallas as pl
from jax.experimental.pallas import tpu as pltpu
from jax.sharding import PartitionSpec as P

Q = 128
MESH = pl.DeviceIdType.MESH
OWN, XSIDE, YSIDE, DIAG = range(4)
ACT, GRAD = range(2)

LIMIT = 60 * 1024 * 1024

CHUNK_TIME = 1.4
HOP_TIME = 1.7
POLL_TIME = 0.5
LOAD_TIME = 3.0
UNIT_TIME = 1.0


def route_blocks(line, layers):
    reach = (2 + line) // 3
    even = line % 2 == 0
    free, events, log = {}, [], [[] for _ in range(line)]

    def flipped(at):
        return even and 2 * at > line - 1

    def send(time, at, route, chunk):
        start = max(free.get((at, route), 0.0), time)
        free[at, route] = start + CHUNK_TIME
        there = at + {"x": 0, "y": 0, "up": 1, "down": -1}[route]
        column, plane, which, layer = chunk
        seen = line - 1 - plane if flipped(there) else plane
        role = line - 1 - there if flipped(there) else there
        key = (round(start + CHUNK_TIME + HOP_TIME, 3), role, seen, column, layer, which, there)
        heapq.heappush(events, (key, chunk))

    def passes(at, chunk):
        column, plane, which, layer = chunk
        along = []
        if plane <= at < line - 1:
            along.append(("up", at + 1))
        if plane >= at > 0:
            along.append(("down", at - 1))
        if flipped(at):
            along.reverse()
        distance = abs(plane - at)
        far = distance > reach
        out = []
        if column == OWN:
            out += [(route, chunk) for route, _ in along]
            if plane != at:
                out.append(("y", (YSIDE, plane, which, layer)))
                late = far and layer == layers - 1
                if which == GRAD or not late:
                    out.append(("x", (XSIDE, plane, which, layer)))
                if which == GRAD and late:
                    out.append(("x", (XSIDE, plane, ACT, layer)))
        if column == DIAG:
            out += [(route, chunk) for route, to in along if abs(plane - to) <= reach]
        if far or distance == 0:
            if column == YSIDE and which == ACT:
                out.append(("x", (DIAG, plane, which, layer)))
            if column == XSIDE and which == GRAD:
                out.append(("y", (DIAG, plane, which, layer)))
        return out

    first = []
    for at in range(line):
        mine = []
        for i in range(2 * layers):
            mine += passes(at, (OWN, at, i % 2, i // 2))
            mine.append(("x", (XSIDE, at, 1 - i // layers, i % layers)))
            mine.append(("y", (YSIDE, at, i // layers, i % layers)))
        for route, chunk in mine:
            send(0.0, at, route, chunk)
        first.append(mine)
    while events:
        (time, *_, at), chunk = heapq.heappop(events)
        out = passes(at, chunk)
        for route, sent in out:
            send(time + POLL_TIME, at, route, sent)
        log[at].append((time, chunk, out))
    return first, log


def plan_steps(at, line, layers, log):
    ready = {(OWN, at, layer): 0.0 for layer in range(layers)}
    for time, (column, plane, _, layer), _ in log:
        ready[column, plane, layer] = max(time, ready.get((column, plane, layer), 0.0))
    blocks = sorted(
        {key[:2] for key in ready}, key=lambda b: [ready[(*b, l)] for l in range(layers)][::-1]
    )
    units = []
    for one, two in zip(blocks[::2], blocks[1::2]):
        for layer in range(layers):
            units.append((max(ready[(*one, layer)], ready[(*two, layer)]), one, two, layer))
    units.sort(key=lambda unit: unit[0])
    steps, now, i = [], LOAD_TIME, 0
    for k, (time, one, two, layer) in enumerate(units):
        now = max(now, time)
        moves = []
        while i < len(log) and (log[i][0] <= now + 0.8 or k == len(units) - 1):
            moves.append(log[i][1:])
            now = max(now, log[i][0])
            i += 1
        steps.append((moves, one, two, layer))
        now += UNIT_TIME
    return steps


def branch(value, low, high, leaf):
    if high - low == 1:
        leaf(low)
        return
    middle = (low + high) // 2
    pl.when(value < middle)(lambda: branch(value, low, middle, leaf))
    pl.when(value >= middle)(lambda: branch(value, middle, high, leaf))


def pick(index, values):
    result = jnp.int32(values[-1])
    for i, value in enumerate(values[:-1]):
        result = jnp.where(index == i, jnp.int32(value), result)
    return result


def kernel(
    layers,
    line,
    train_a,
    train_g,
    test_a,
    test_g,
    ids_hbm,
    out_ref,
    ids_ref,
    prod,
    ta,
    tg,
    buf,
    acc,
    xbuf,
    xout,
    train_sem,
    own_sem,
    recv_sem,
    send_sem,
    xs_sem,
    xr_sem,
):
    me = lax.axis_index("tok")
    core = lax.axis_index("layer")
    z = me // 4
    y = (me // 2) % 2
    x = me % 2
    columns = (
        y * 2 + x,
        y * 2 + (1 - x),
        (1 - y) * 2 + x,
        (1 - y) * 2 + (1 - x),
    )
    layer_count, train_rows, _ = ta.shape
    _, rows, width = buf.shape
    q_block = Q // layers
    has_up = z < line - 1
    has_down = z > 0

    roles = line // 2 if line % 2 == 0 else line
    flip = (z >= roles).astype(jnp.int32)
    role = jnp.where(flip == 1, line - 1 - z, z)
    sign = 1 - 2 * flip
    partner = {
        "x": z * 4 + columns[XSIDE],
        "y": z * 4 + columns[YSIDE],
        "up": me + 4 * sign,
        "down": me - 4 * sign,
    }
    routes = tuple(partner)
    across = {
        "x": (XSIDE, OWN, DIAG, YSIDE),
        "y": (YSIDE, DIAG, OWN, XSIDE),
        "up": (OWN, XSIDE, YSIDE, DIAG),
        "down": (OWN, XSIDE, YSIDE, DIAG),
    }

    def place(column, plane):
        return jnp.where(flip == 1, line - 1 - plane, plane) * 4 + columns[column]

    def slot(column, plane, which, layer):
        return (place(column, plane) * layer_count + layer) * 2 + which


    def own_copy(which, layer):
        src = (test_a, test_g)[which]
        return pltpu.make_async_copy(
            src.at[layer],
            buf.at[(me * layer_count + layer) * 2 + which],
            own_sem.at[which, layer],
        )

    for which in range(2):
        for layer in range(layer_count):
            own_copy(which, layer).start()
    ids_copy = pltpu.make_async_copy(ids_hbm, ids_ref, train_sem.at[2])
    ids_copy.start()

    barrier = pltpu.get_barrier_semaphore()

    def greet(where):
        pl.semaphore_signal(barrier, inc=1, device_id=where, device_id_type=MESH)

    greet({"tok": partner["x"]})
    greet({"tok": partner["y"]})
    pl.when(has_up)(lambda: greet({"tok": me + 4}))
    pl.when(has_down)(lambda: greet({"tok": me - 4}))
    for step in range(1, layers):
        greet({"layer": lax.rem(core + step, layers)})
    ends = jnp.where(has_up, 1, 0) + jnp.where(has_down, 1, 0)
    pl.semaphore_wait(barrier, layers + 1 + ends)

    def copy(route, chunk, src=None):
        column, plane, which, layer = chunk
        here = slot(across[route][column], plane, which, layer)
        return pltpu.make_async_remote_copy(
            src_ref=buf.at[here] if src is None else src,
            dst_ref=buf.at[here],
            send_sem=send_sem.at[routes.index(route)],
            recv_sem=recv_sem.at[here],
            device_id={"tok": partner[route]},
            device_id_type=MESH,
        )

    def arrived(chunk):
        here = slot(*chunk)
        pltpu.make_async_remote_copy(
            src_ref=buf.at[here],
            dst_ref=buf.at[here],
            send_sem=send_sem.at[0],
            recv_sem=recv_sem.at[here],
            device_id={"tok": partner["x"]},
            device_id_type=MESH,
        ).wait_recv()

    first, log = route_blocks(line, layer_count)
    steps = [plan_steps(at, line, layer_count, log[at]) for at in range(roles)]
    count = len(steps[0])

    def send_own(at):
        for route, chunk in first[at]:
            copy(route, chunk, (test_a, test_g)[chunk[2]].at[chunk[3]]).start()

    branch(role, 0, roles, send_own)

    for which, (src, dst) in enumerate(((train_a, ta), (train_g, tg))):
        pltpu.make_async_copy(src, dst, train_sem.at[which]).start()

    acc[...] = jnp.zeros_like(acc)
    _, tiles, _, tile = xbuf.shape
    labels = lax.broadcasted_iota(jnp.int32, (Q, rows), 0)
    nt = (((1,), (1,)), ((), ()))

    def exchange(step, j):
        to = lax.rem(core + step, layers)
        return pltpu.make_async_remote_copy(
            src_ref=xout.at[step - 1, j],
            dst_ref=xbuf.at[step - 1, j],
            send_sem=xs_sem.at[step - 1, j],
            recv_sem=xr_sem.at[step - 1, j],
            device_id={"layer": to},
            device_id_type=MESH,
        )

    ids_copy.wait()
    for which in range(2):
        for layer in range(layer_count):
            own_copy(which, layer).wait()
    for which, (src, dst) in enumerate(((train_a, ta), (train_g, tg))):
        pltpu.make_async_copy(src, dst, train_sem.at[which]).wait()

    def relay(k, at):
        for chunk, out in steps[at][k][0]:
            arrived(chunk)
            for route, sent in out:
                copy(route, sent).start()

    base = line * 4
    packed = [
        (
            ((one[1] * 4 + one[0]) * base + two[1] * 4 + two[0]) * layer_count + layer
        )
        for at in range(roles)
        for _, one, two, layer in steps[at]
    ]

    def position(code):
        plane, column = code // 4, code % 4
        plane = jnp.where(flip == 1, line - 1 - plane, plane)
        return plane * 4 + pick(column, columns)

    def step(k, carry):
        branch(k, 0, count, lambda k0: branch(role, 0, roles, functools.partial(relay, k0)))
        code = pick(role * count + k, packed)
        layer = code % layer_count
        one = position(code // layer_count // base)
        two = position((code // layer_count) % base)
        select = jnp.concatenate(
            [
                jnp.where(ids_ref[b] == labels, 1.0, 0.0).astype(jnp.bfloat16)
                for b in (one, two)
            ],
            axis=1,
        )

        def held(which):
            return jnp.concatenate(
                [buf[(b * layer_count + layer) * 2 + which] for b in (one, two)], axis=0
            )

        a_held, g_held = held(ACT), held(GRAD)
        one_q = jnp.where(ids_ref[one] == labels, 1.0, 0.0).astype(jnp.bfloat16)

        a_gram = lax.dot_general(a_held, ta[layer], nt, preferred_element_type=jnp.float32)
        g_gram = lax.dot_general(g_held, tg[layer], nt, preferred_element_type=jnp.float32)
        prod[...] = (a_gram * g_gram).astype(jnp.bfloat16)

        acc[...] += jnp.dot(select, prod[...], preferred_element_type=jnp.float32)

        @pl.when(k == count - 1)
        def _():
            for j in range(tiles):
                for step in range(1, layers):
                    theirs = lax.rem(core + step, layers) * q_block
                    xout[step - 1, j] = acc[
                        pl.ds(pl.multiple_of(theirs, q_block), q_block), pl.ds(j * tile, tile)
                    ].astype(jnp.bfloat16)
                    exchange(step, j).start()
        return carry

    lax.fori_loop(0, count, step, 0)

    def drain(at):
        sent = list(first[at])
        for moves, *_ in steps[at]:
            for _, out in moves:
                sent += out
        for i, route in enumerate(routes):
            total = sum(r == route for r, _ in sent)
            if total > 0:
                all_of_them = buf.at[pl.ds(0, total)]
                pltpu.make_async_remote_copy(
                    src_ref=all_of_them,
                    dst_ref=all_of_them,
                    send_sem=send_sem.at[i],
                    recv_sem=recv_sem.at[0],
                    device_id={"tok": partner["x"]},
                    device_id_type=MESH,
                ).wait_send()

    branch(role, 0, roles, drain)

    mine = pl.ds(pl.multiple_of(core * q_block, q_block), q_block)
    for j in range(tiles):
        at = pl.ds(j * tile, tile)
        for step in range(1, layers):
            exchange(step, j).wait_recv()
        result = acc[mine, at]
        for step in range(1, layers):
            result = result + xbuf[step - 1, j].astype(jnp.float32)
        out_ref[:, at] = result
    for j in range(tiles):
        for step in range(1, layers):
            exchange(step, j).wait_send()


def on_device(layers, toks, train_act, train_grad, test_act, test_grad, segment_ids):
    layer_count, train_rows, width = train_act.shape
    rows = test_act.shape[1]
    line = toks // 4
    tile = math.gcd(train_rows, 1024)
    tiles = train_rows // tile
    q_block = Q // layers
    ids = segment_ids.reshape(toks, 1, rows)
    dma = pltpu.SemaphoreType.DMA
    in_hbm = pl.BlockSpec(memory_space=pltpu.HBM)
    return pl.pallas_call(
        functools.partial(kernel, layers, line),
        out_shape=pltpu.VMEM((q_block, train_rows), jnp.float32),
        in_specs=[in_hbm] * 5,
        out_specs=pl.BlockSpec(memory_space=pltpu.VMEM),
        scratch_shapes=[
            pltpu.VMEM((toks, 1, rows), jnp.int32),
            pltpu.VMEM((2 * rows, train_rows), jnp.bfloat16),
            pltpu.VMEM((layer_count, train_rows, width), jnp.bfloat16),
            pltpu.VMEM((layer_count, train_rows, width), jnp.bfloat16),
            pltpu.VMEM((toks * layer_count * 2, rows, width), jnp.bfloat16),
            pltpu.VMEM((Q, train_rows), jnp.float32),
            pltpu.VMEM((layers - 1, tiles, q_block, tile), jnp.bfloat16),
            pltpu.VMEM((layers - 1, tiles, q_block, tile), jnp.bfloat16),
            dma((3,)),
            dma((2, layer_count)),
            dma((toks * layer_count * 2,)),
            dma((4,)),
            dma((layers - 1, tiles)),
            dma((layers - 1, tiles)),
        ],
        compiler_params=pltpu.CompilerParams(
            collective_id=0, has_side_effects=True, vmem_limit_bytes=LIMIT
        ),
    )(train_act, train_grad, test_act, test_grad, ids)


def solution(mesh):
    placed = (
        P("layer", "tok", None),
        P("layer", "tok", None),
        P("layer", "tok", None),
        P("layer", "tok", None),
        P(),
    )
    body = functools.partial(on_device, mesh.shape["layer"], mesh.shape["tok"])
    return jax.shard_map(
        body, mesh=mesh, in_specs=placed, out_specs=P("layer", "tok"), check_vma=False
    )
```

```python
import functools
import heapq
import math

import jax
import jax.numpy as jnp
from jax import lax
from jax.experimental import pallas as pl
from jax.experimental.pallas import tpu as pltpu
from jax.sharding import PartitionSpec as P

Q = 128
MESH = pl.DeviceIdType.MESH
OWN, XSIDE, YSIDE, DIAG = range(4)
ACT, GRAD = range(2)

LIMIT = 60 * 1024 * 1024

CHUNK_TIME = 1.4
HOP_TIME = 1.7
POLL_TIME = 0.5
GROUP_TIME = 0.3
AHEAD_TIME = 0.8
LOAD_TIME = 3.0
UNIT_TIME = 1.0


def route_blocks(line, layers):
    reach = (2 + line) // 3
    even = line % 2 == 0
    free, events, log = {}, [], [[] for _ in range(line)]

    def flipped(at):
        return even and 2 * at > line - 1

    def send(time, at, route, chunk):
        start = max(free.get((at, route), 0.0), time)
        free[at, route] = start + CHUNK_TIME
        there = at + {"x": 0, "y": 0, "up": 1, "down": -1}[route]
        column, plane, which, layer = chunk
        seen = line - 1 - plane if flipped(there) else plane
        role = line - 1 - there if flipped(there) else there
        key = (round(start + CHUNK_TIME + HOP_TIME, 3), role, seen, column, layer, which, there)
        heapq.heappush(events, (key, chunk))

    def passes(at, chunk):
        column, plane, which, layer = chunk
        along = []
        if plane <= at < line - 1:
            along.append(("up", at + 1))
        if plane >= at > 0:
            along.append(("down", at - 1))
        if flipped(at):
            along.reverse()
        distance = abs(plane - at)
        far = distance > reach
        out = []
        if column == OWN:
            out += [(route, chunk) for route, _ in along]
            if plane != at:
                out.append(("y", (YSIDE, plane, which, layer)))
                late = far and layer == layers - 1
                if which == GRAD or not late:
                    out.append(("x", (XSIDE, plane, which, layer)))
                if which == GRAD and late:
                    out.append(("x", (XSIDE, plane, ACT, layer)))
        if column == DIAG:
            out += [(route, chunk) for route, to in along if abs(plane - to) <= reach]
        if far or distance == 0:
            if column == YSIDE and which == ACT:
                out.append(("x", (DIAG, plane, which, layer)))
            if column == XSIDE and which == GRAD:
                out.append(("y", (DIAG, plane, which, layer)))
        return out

    first = []
    for at in range(line):
        mine = []
        for i in range(2 * layers):
            mine += passes(at, (OWN, at, i % 2, i // 2))
            mine.append(("x", (XSIDE, at, 1 - i // layers, i % layers)))
            mine.append(("y", (YSIDE, at, i // layers, i % layers)))
        for route, chunk in mine:
            send(0.0, at, route, chunk)
        first.append(mine)
    while events:
        (time, *_, at), chunk = heapq.heappop(events)
        out = passes(at, chunk)
        for route, sent in out:
            send(time + POLL_TIME, at, route, sent)
        log[at].append((time, chunk, out))
    return first, log


def gather_groups(log):
    groups, opened = [], 0.0
    for time, chunk, out in log:
        if not groups or time > opened + GROUP_TIME:
            groups.append([])
            opened = time
        groups[-1].append((time, chunk, out))
    return groups


def plan_steps(at, layers, groups):
    ready = {(OWN, at, layer): 0.0 for layer in range(layers)}
    for group in groups:
        for _, (column, plane, _, layer), _ in group:
            ready[column, plane, layer] = group[-1][0]
    blocks = sorted(
        {key[:2] for key in ready}, key=lambda b: [ready[(*b, l)] for l in range(layers)][::-1]
    )
    units = []
    for one, two in zip(blocks[::2], blocks[1::2]):
        for layer in range(layers):
            units.append((max(ready[(*one, layer)], ready[(*two, layer)]), one, two, layer))
    units.sort(key=lambda unit: unit[0])
    steps, now, i = [], LOAD_TIME, 0
    for k, (time, one, two, layer) in enumerate(units):
        now = max(now, time)
        moves = []
        while i < len(groups) and (
            groups[i][-1][0] <= now + AHEAD_TIME or k == len(units) - 1
        ):
            now = max(now, groups[i][-1][0])
            moves.append(i)
            i += 1
        steps.append((moves, one, two, layer))
        now += UNIT_TIME
    return steps


def branch(value, low, high, leaf):
    if high - low == 1:
        leaf(low)
        return
    middle = (low + high) // 2
    pl.when(value < middle)(lambda: branch(value, low, middle, leaf))
    pl.when(value >= middle)(lambda: branch(value, middle, high, leaf))


def pick(index, values):
    result = jnp.int32(values[-1])
    for i, value in enumerate(values[:-1]):
        result = jnp.where(index == i, jnp.int32(value), result)
    return result


def kernel(
    layers,
    line,
    first,
    groups,
    train_a,
    train_g,
    test_a,
    test_g,
    ids_hbm,
    out_ref,
    ids_ref,
    prod,
    train,
    buf,
    acc,
    xbuf,
    xout,
    train_sem,
    own_sem,
    recv_sem,
    send_sem,
    xs_sem,
    xr_sem,
):
    me = lax.axis_index("tok")
    core = lax.axis_index("layer")
    z = me // 4
    y = (me // 2) % 2
    x = me % 2
    columns = (
        y * 2 + x,
        y * 2 + (1 - x),
        (1 - y) * 2 + x,
        (1 - y) * 2 + (1 - x),
    )
    _, layer_count, train_rows, _ = train.shape
    _, rows, width = buf.shape
    q_block = Q // layers
    has_up = z < line - 1
    has_down = z > 0

    roles = line // 2 if line % 2 == 0 else line
    flip = (z >= roles).astype(jnp.int32)
    role = jnp.where(flip == 1, line - 1 - z, z)
    sign = 1 - 2 * flip
    partner = {
        "x": z * 4 + columns[XSIDE],
        "y": z * 4 + columns[YSIDE],
        "up": me + 4 * sign,
        "down": me - 4 * sign,
    }
    routes = tuple(partner)
    group_of = [
        {chunk: i for i, group in enumerate(groups[at]) for _, chunk, _ in group}
        for at in range(roles)
    ]

    def group_there(at, route, chunk):
        column, plane, which, layer = chunk
        there = at + {"x": 0, "y": 0, "up": 1, "down": -1}[route]
        if there >= roles:
            there, plane = line - 1 - there, line - 1 - plane
        return group_of[there][column, plane, which, layer]

    across = {
        "x": (XSIDE, OWN, DIAG, YSIDE),
        "y": (YSIDE, DIAG, OWN, XSIDE),
        "up": (OWN, XSIDE, YSIDE, DIAG),
        "down": (OWN, XSIDE, YSIDE, DIAG),
    }

    def place(column, plane):
        return jnp.where(flip == 1, line - 1 - plane, plane) * 4 + columns[column]

    def slot(column, plane, which, layer):
        return (place(column, plane) * layer_count + layer) * 2 + which


    def own_copy(which, layer):
        src = (test_a, test_g)[which]
        return pltpu.make_async_copy(
            src.at[layer],
            buf.at[(me * layer_count + layer) * 2 + which],
            own_sem.at[0],
        )

    for which in range(2):
        for layer in range(layer_count):
            own_copy(which, layer).start()
    ids_copy = pltpu.make_async_copy(ids_hbm, ids_ref, train_sem.at[1])
    ids_copy.start()

    barrier = pltpu.get_barrier_semaphore()

    def greet(where):
        pl.semaphore_signal(barrier, inc=1, device_id=where, device_id_type=MESH)

    greet({"tok": partner["x"]})
    greet({"tok": partner["y"]})
    pl.when(has_up)(lambda: greet({"tok": me + 4}))
    pl.when(has_down)(lambda: greet({"tok": me - 4}))
    for step in range(1, layers):
        greet({"layer": lax.rem(core + step, layers)})
    ends = jnp.where(has_up, 1, 0) + jnp.where(has_down, 1, 0)
    pl.semaphore_wait(barrier, layers + 1 + ends)

    def copy(at, route, chunk, src=None):
        column, plane, which, layer = chunk
        here = slot(across[route][column], plane, which, layer)
        return pltpu.make_async_remote_copy(
            src_ref=buf.at[here] if src is None else src,
            dst_ref=buf.at[here],
            send_sem=send_sem.at[routes.index(route)],
            recv_sem=recv_sem.at[group_there(at, route, chunk)],
            device_id={"tok": partner[route]},
            device_id_type=MESH,
        )

    def arrived(index, size):
        pltpu.make_async_remote_copy(
            src_ref=buf.at[pl.ds(0, size)],
            dst_ref=buf.at[pl.ds(0, size)],
            send_sem=send_sem.at[0],
            recv_sem=recv_sem.at[index],
            device_id={"tok": partner["x"]},
            device_id_type=MESH,
        ).wait_recv()

    steps = [plan_steps(at, layer_count, groups[at]) for at in range(roles)]
    count = len(steps[0])

    def send_own(at):
        for route, chunk in first[at]:
            copy(at, route, chunk, (test_a, test_g)[chunk[2]].at[chunk[3]]).start()

    branch(role, 0, roles, send_own)

    for which, src in enumerate((train_a, train_g)):
        pltpu.make_async_copy(src, train.at[which], train_sem.at[0]).start()

    acc[...] = jnp.zeros_like(acc)
    _, tiles, _, tile = xbuf.shape
    labels = lax.broadcasted_iota(jnp.int32, (Q, rows), 0)
    nt = (((1,), (1,)), ((), ()))

    def exchange(step, j):
        to = lax.rem(core + step, layers)
        return pltpu.make_async_remote_copy(
            src_ref=xout.at[step - 1, j],
            dst_ref=xbuf.at[step - 1, j],
            send_sem=xs_sem.at[step - 1, j],
            recv_sem=xr_sem.at[step - 1, j],
            device_id={"layer": to},
            device_id_type=MESH,
        )

    ids_copy.wait()
    own_all = buf.at[pl.ds(me * layer_count * 2, layer_count * 2)]
    pltpu.make_async_copy(own_all, own_all, own_sem.at[0]).wait()
    pltpu.make_async_copy(train, train, train_sem.at[0]).wait()

    def relay(k, at):
        for index in steps[at][k][0]:
            group = groups[at][index]
            arrived(index, len(group))
            for _, _, out in group:
                for route, sent in out:
                    copy(at, route, sent).start()

    base = line * 4
    packed = [
        (
            ((one[1] * 4 + one[0]) * base + two[1] * 4 + two[0]) * layer_count + layer
        )
        for at in range(roles)
        for _, one, two, layer in steps[at]
    ]

    def position(code):
        plane, column = code // 4, code % 4
        plane = jnp.where(flip == 1, line - 1 - plane, plane)
        return plane * 4 + pick(column, columns)

    def step(k, carry):
        branch(k, 0, count, lambda k0: branch(role, 0, roles, functools.partial(relay, k0)))
        code = pick(role * count + k, packed)
        layer = code % layer_count
        one = position(code // layer_count // base)
        two = position((code // layer_count) % base)
        select = jnp.concatenate(
            [
                jnp.where(ids_ref[b] == labels, 1.0, 0.0).astype(jnp.bfloat16)
                for b in (one, two)
            ],
            axis=1,
        )

        def held(which):
            return jnp.concatenate(
                [buf[(b * layer_count + layer) * 2 + which] for b in (one, two)], axis=0
            )

        a_held, g_held = held(ACT), held(GRAD)
        one_q = jnp.where(ids_ref[one] == labels, 1.0, 0.0).astype(jnp.bfloat16)

        a_gram = lax.dot_general(a_held, train[ACT, layer], nt, preferred_element_type=jnp.float32)
        g_gram = lax.dot_general(g_held, train[GRAD, layer], nt, preferred_element_type=jnp.float32)
        prod[...] = (a_gram * g_gram).astype(jnp.bfloat16)

        acc[...] += jnp.dot(select, prod[...], preferred_element_type=jnp.float32)

        @pl.when(k == count - 1)
        def _():
            for j in range(tiles):
                for step in range(1, layers):
                    theirs = lax.rem(core + step, layers) * q_block
                    xout[step - 1, j] = acc[
                        pl.ds(pl.multiple_of(theirs, q_block), q_block), pl.ds(j * tile, tile)
                    ].astype(jnp.bfloat16)
                    exchange(step, j).start()
        return carry

    lax.fori_loop(0, count, step, 0)

    def drain(at):
        sent = list(first[at])
        for group in groups[at]:
            for _, _, out in group:
                sent += out
        for i, route in enumerate(routes):
            total = sum(r == route for r, _ in sent)
            if total > 0:
                all_of_them = buf.at[pl.ds(0, total)]
                pltpu.make_async_remote_copy(
                    src_ref=all_of_them,
                    dst_ref=all_of_them,
                    send_sem=send_sem.at[i],
                    recv_sem=recv_sem.at[0],
                    device_id={"tok": partner["x"]},
                    device_id_type=MESH,
                ).wait_send()

    branch(role, 0, roles, drain)

    mine = pl.ds(pl.multiple_of(core * q_block, q_block), q_block)
    for j in range(tiles):
        at = pl.ds(j * tile, tile)
        for step in range(1, layers):
            exchange(step, j).wait_recv()
        result = acc[mine, at]
        for step in range(1, layers):
            result = result + xbuf[step - 1, j].astype(jnp.float32)
        out_ref[:, at] = result
    for j in range(tiles):
        for step in range(1, layers):
            exchange(step, j).wait_send()


def on_device(layers, toks, train_act, train_grad, test_act, test_grad, segment_ids):
    layer_count, train_rows, width = train_act.shape
    rows = test_act.shape[1]
    line = toks // 4
    first, log = route_blocks(line, layer_count)
    groups = [gather_groups(received) for received in log]
    tile = math.gcd(train_rows, 2048)
    tiles = train_rows // tile
    q_block = Q // layers
    ids = segment_ids.reshape(toks, 1, rows)
    dma = pltpu.SemaphoreType.DMA
    in_hbm = pl.BlockSpec(memory_space=pltpu.HBM)
    return pl.pallas_call(
        functools.partial(kernel, layers, line, first, groups),
        out_shape=pltpu.VMEM((q_block, train_rows), jnp.float32),
        in_specs=[in_hbm] * 5,
        out_specs=pl.BlockSpec(memory_space=pltpu.VMEM),
        scratch_shapes=[
            pltpu.VMEM((toks, 1, rows), jnp.int32),
            pltpu.VMEM((2 * rows, train_rows), jnp.bfloat16),
            pltpu.VMEM((2, layer_count, train_rows, width), jnp.bfloat16),
            pltpu.VMEM((toks * layer_count * 2, rows, width), jnp.bfloat16),
            pltpu.VMEM((Q, train_rows), jnp.float32),
            pltpu.VMEM((layers - 1, tiles, q_block, tile), jnp.bfloat16),
            pltpu.VMEM((layers - 1, tiles, q_block, tile), jnp.bfloat16),
            dma((2,)),
            dma((1,)),
            dma((max(len(g) for g in groups),)),
            dma((4,)),
            dma((layers - 1, tiles)),
            dma((layers - 1, tiles)),
        ],
        compiler_params=pltpu.CompilerParams(
            collective_id=0, has_side_effects=True, vmem_limit_bytes=LIMIT
        ),
    )(train_act, train_grad, test_act, test_grad, ids)


def solution(mesh):
    placed = (
        P("layer", "tok", None),
        P("layer", "tok", None),
        P("layer", "tok", None),
        P("layer", "tok", None),
        P(),
    )
    body = functools.partial(on_device, mesh.shape["layer"], mesh.shape["tok"])
    return jax.shard_map(
        body, mesh=mesh, in_specs=placed, out_specs=P("layer", "tok"), check_vma=False
    )
```

```python
import functools
import heapq
import math

import jax
import jax.numpy as jnp
from jax import lax
from jax.experimental import pallas as pl
from jax.experimental.pallas import tpu as pltpu
from jax.sharding import PartitionSpec as P

Q = 128
MESH = pl.DeviceIdType.MESH
OWN, XSIDE, YSIDE, DIAG = range(4)
ACT, GRAD = range(2)

LIMIT = 60 * 1024 * 1024

CHUNK_TIME = 1.4
HOP_TIME = 1.7
POLL_TIME = 0.5
GROUP_TIME = 0.3
AHEAD_TIME = 0.8
LOAD_TIME = 3.0
UNIT_TIME = 1.0


def route_blocks(line, layers):
    reach = (2 + line) // 3
    even = line % 2 == 0
    free, events, log = {}, [], [[] for _ in range(line)]

    def flipped(at):
        return even and 2 * at > line - 1

    def send(time, at, route, chunk):
        start = max(free.get((at, route), 0.0), time)
        free[at, route] = start + CHUNK_TIME
        there = at + {"x": 0, "y": 0, "up": 1, "down": -1}[route]
        column, plane, which, layer = chunk
        seen = line - 1 - plane if flipped(there) else plane
        role = line - 1 - there if flipped(there) else there
        key = (round(start + CHUNK_TIME + HOP_TIME, 3), role, seen, column, layer, which, there)
        heapq.heappush(events, (key, chunk))

    def passes(at, chunk):
        column, plane, which, layer = chunk
        along = []
        if plane <= at < line - 1:
            along.append(("up", at + 1))
        if plane >= at > 0:
            along.append(("down", at - 1))
        if flipped(at):
            along.reverse()
        distance = abs(plane - at)
        far = distance > reach
        out = []
        if column == OWN:
            out += [(route, chunk) for route, _ in along]
            if plane != at:
                out.append(("y", (YSIDE, plane, which, layer)))
                late = far and layer == layers - 1
                if which == GRAD or not late:
                    out.append(("x", (XSIDE, plane, which, layer)))
                if which == GRAD and late:
                    out.append(("x", (XSIDE, plane, ACT, layer)))
        if column == DIAG:
            out += [(route, chunk) for route, to in along if abs(plane - to) <= reach]
        if far or distance == 0:
            if column == YSIDE and which == ACT:
                out.append(("x", (DIAG, plane, which, layer)))
            if column == XSIDE and which == GRAD:
                out.append(("y", (DIAG, plane, which, layer)))
        return out

    first = []
    for at in range(line):
        mine = []
        for i in range(2 * layers):
            mine += passes(at, (OWN, at, i % 2, i // 2))
            mine.append(("x", (XSIDE, at, 1 - i // layers, i % layers)))
            mine.append(("y", (YSIDE, at, i // layers, i % layers)))
        for route, chunk in mine:
            send(0.0, at, route, chunk)
        first.append(mine)
    while events:
        (time, *_, at), chunk = heapq.heappop(events)
        out = passes(at, chunk)
        for route, sent in out:
            send(time + POLL_TIME, at, route, sent)
        log[at].append((time, chunk, out))
    return first, log


def gather_groups(log):
    groups, opened = [], 0.0
    for time, chunk, out in log:
        if not groups or time > opened + GROUP_TIME:
            groups.append([])
            opened = time
        groups[-1].append((time, chunk, out))
    return groups


def plan_steps(at, layers, groups):
    ready = {(OWN, at, layer): 0.0 for layer in range(layers)}
    for group in groups:
        for _, (column, plane, _, layer), _ in group:
            ready[column, plane, layer] = group[-1][0]
    blocks = sorted(
        {key[:2] for key in ready}, key=lambda b: [ready[(*b, l)] for l in range(layers)][::-1]
    )
    units = []
    for one, two in zip(blocks[::2], blocks[1::2]):
        for layer in range(layers):
            units.append((max(ready[(*one, layer)], ready[(*two, layer)]), one, two, layer))
    units.sort(key=lambda unit: unit[0])
    steps, now, i = [], LOAD_TIME, 0
    for k, (time, one, two, layer) in enumerate(units):
        now = max(now, time)
        moves = []
        while i < len(groups) and (
            groups[i][-1][0] <= now + AHEAD_TIME or k == len(units) - 1
        ):
            now = max(now, groups[i][-1][0])
            moves.append(i)
            i += 1
        steps.append((moves, one, two, layer))
        now += UNIT_TIME
    return steps


def branch(value, low, high, leaf):
    if high - low == 1:
        leaf(low)
        return
    middle = (low + high) // 2
    pl.when(value < middle)(lambda: branch(value, low, middle, leaf))
    pl.when(value >= middle)(lambda: branch(value, middle, high, leaf))


def pick(index, values):
    result = jnp.int32(values[-1])
    for i, value in enumerate(values[:-1]):
        result = jnp.where(index == i, jnp.int32(value), result)
    return result


def kernel(
    layers,
    line,
    first,
    groups,
    train_a,
    train_g,
    test_a,
    test_g,
    ids_hbm,
    out_ref,
    ids_ref,
    prod,
    train,
    buf,
    acc,
    xbuf,
    xout,
    train_sem,
    own_sem,
    recv_sem,
    send_sem,
    ready_sem,
    xs_sem,
    xr_sem,
):
    me = lax.axis_index("tok")
    core = lax.axis_index("layer")
    z = me // 4
    y = (me // 2) % 2
    x = me % 2
    columns = (
        y * 2 + x,
        y * 2 + (1 - x),
        (1 - y) * 2 + x,
        (1 - y) * 2 + (1 - x),
    )
    _, layer_count, train_rows, _ = train.shape
    _, rows, width = buf.shape
    q_block = Q // layers
    has_up = z < line - 1
    has_down = z > 0

    roles = line // 2 if line % 2 == 0 else line
    flip = (z >= roles).astype(jnp.int32)
    role = jnp.where(flip == 1, line - 1 - z, z)
    sign = 1 - 2 * flip
    partner = {
        "x": z * 4 + columns[XSIDE],
        "y": z * 4 + columns[YSIDE],
        "up": me + 4 * sign,
        "down": me - 4 * sign,
    }
    routes = tuple(partner)
    group_of = [
        {chunk: i for i, group in enumerate(groups[at]) for _, chunk, _ in group}
        for at in range(roles)
    ]

    def group_there(at, route, chunk):
        column, plane, which, layer = chunk
        there = at + {"x": 0, "y": 0, "up": 1, "down": -1}[route]
        if there >= roles:
            there, plane = line - 1 - there, line - 1 - plane
        return group_of[there][column, plane, which, layer]

    across = {
        "x": (XSIDE, OWN, DIAG, YSIDE),
        "y": (YSIDE, DIAG, OWN, XSIDE),
        "up": (OWN, XSIDE, YSIDE, DIAG),
        "down": (OWN, XSIDE, YSIDE, DIAG),
    }

    def place(column, plane):
        return jnp.where(flip == 1, line - 1 - plane, plane) * 4 + columns[column]

    def slot(column, plane, which, layer):
        return (place(column, plane) * layer_count + layer) * 2 + which


    def own_copy(which, layer):
        src = (test_a, test_g)[which]
        return pltpu.make_async_copy(
            src.at[layer],
            buf.at[(me * layer_count + layer) * 2 + which],
            own_sem.at[0],
        )

    for which in range(2):
        for layer in range(layer_count):
            own_copy(which, layer).start()
    ids_copy = pltpu.make_async_copy(ids_hbm, ids_ref, train_sem.at[1])
    ids_copy.start()

    lower = {"x": x == 1, "y": y == 1, "up": flip == 1, "down": flip == 0}
    axis = {"x": 0, "y": 1, "up": 2, "down": 2}
    barrier = pltpu.get_barrier_semaphore()

    def greet(where, semaphore=barrier):
        pl.semaphore_signal(semaphore, inc=1, device_id=where, device_id_type=MESH)

    pl.when(x == 0)(lambda: greet({"tok": partner["x"]}))
    pl.when(y == 0)(lambda: greet({"tok": partner["y"]}))
    pl.when(has_up)(lambda: greet({"tok": me + 4}))
    for step in range(1, layers):
        greet({"layer": lax.rem(core + step, layers)})
    pl.semaphore_wait(barrier, layers - 1 + x + y + has_down.astype(jnp.int32))
    pl.when(x == 1)(lambda: greet({"tok": partner["x"]}, ready_sem.at[0]))
    pl.when(y == 1)(lambda: greet({"tok": partner["y"]}, ready_sem.at[1]))
    pl.when(has_down)(lambda: greet({"tok": me - 4}, ready_sem.at[2]))

    def copy(at, route, chunk, src=None):
        column, plane, which, layer = chunk
        here = slot(across[route][column], plane, which, layer)
        return pltpu.make_async_remote_copy(
            src_ref=buf.at[here] if src is None else src,
            dst_ref=buf.at[here],
            send_sem=send_sem.at[routes.index(route)],
            recv_sem=recv_sem.at[group_there(at, route, chunk)],
            device_id={"tok": partner[route]},
            device_id_type=MESH,
        )

    def arrived(index, size):
        pltpu.make_async_remote_copy(
            src_ref=buf.at[pl.ds(0, size)],
            dst_ref=buf.at[pl.ds(0, size)],
            send_sem=send_sem.at[0],
            recv_sem=recv_sem.at[index],
            device_id={"tok": partner["x"]},
            device_id_type=MESH,
        ).wait_recv()

    steps = [plan_steps(at, layer_count, groups[at]) for at in range(roles)]
    count = len(steps[0])

    def send_own(at):
        def send(route):
            for own_route, chunk in first[at]:
                if own_route == route:
                    src = (test_a, test_g)[chunk[2]].at[chunk[3]]
                    copy(at, route, chunk, src).start()

        def answered(route):
            pl.semaphore_wait(ready_sem.at[axis[route]], 1)
            send(route)

        used = sorted({route for route, _ in first[at]}, key=routes.index)
        for route in used:
            pl.when(lower[route])(functools.partial(send, route))
        for route in used:
            pl.when(jnp.logical_not(lower[route]))(functools.partial(answered, route))

    branch(role, 0, roles, send_own)

    for which, src in enumerate((train_a, train_g)):
        pltpu.make_async_copy(src, train.at[which], train_sem.at[0]).start()

    acc[...] = jnp.zeros_like(acc)
    _, tiles, _, tile = xbuf.shape
    labels = lax.broadcasted_iota(jnp.int32, (Q, rows), 0)
    nt = (((1,), (1,)), ((), ()))

    def exchange(step, j):
        to = lax.rem(core + step, layers)
        return pltpu.make_async_remote_copy(
            src_ref=xout.at[step - 1, j],
            dst_ref=xbuf.at[step - 1, j],
            send_sem=xs_sem.at[step - 1, j],
            recv_sem=xr_sem.at[step - 1, j],
            device_id={"layer": to},
            device_id_type=MESH,
        )

    ids_copy.wait()
    own_all = buf.at[pl.ds(me * layer_count * 2, layer_count * 2)]
    pltpu.make_async_copy(own_all, own_all, own_sem.at[0]).wait()
    pltpu.make_async_copy(train, train, train_sem.at[0]).wait()

    def relay(k, at):
        for index in steps[at][k][0]:
            group = groups[at][index]
            arrived(index, len(group))
            for _, _, out in group:
                for route, sent in out:
                    copy(at, route, sent).start()

    base = line * 4
    packed = [
        (
            ((one[1] * 4 + one[0]) * base + two[1] * 4 + two[0]) * layer_count + layer
        )
        for at in range(roles)
        for _, one, two, layer in steps[at]
    ]

    def position(code):
        plane, column = code // 4, code % 4
        plane = jnp.where(flip == 1, line - 1 - plane, plane)
        return plane * 4 + pick(column, columns)

    def step(k, carry):
        code = pick(role * count + k, packed)
        layer = code % layer_count
        one = position(code // layer_count // base)
        two = position((code // layer_count) % base)
        select = jnp.concatenate(
            [
                jnp.where(ids_ref[b] == labels, 1.0, 0.0).astype(jnp.bfloat16)
                for b in (one, two)
            ],
            axis=1,
        )

        branch(k, 0, count, lambda k0: branch(role, 0, roles, functools.partial(relay, k0)))

        def held(which):
            return jnp.concatenate(
                [buf[(b * layer_count + layer) * 2 + which] for b in (one, two)], axis=0
            )

        a_held, g_held = held(ACT), held(GRAD)

        a_gram = lax.dot_general(a_held, train[ACT, layer], nt, preferred_element_type=jnp.float32)
        g_gram = lax.dot_general(g_held, train[GRAD, layer], nt, preferred_element_type=jnp.float32)
        prod[...] = (a_gram * g_gram).astype(jnp.bfloat16)

        acc[...] += jnp.dot(select, prod[...], preferred_element_type=jnp.float32)

        @pl.when(k == count - 1)
        def _():
            for j in range(tiles):
                for step in range(1, layers):
                    theirs = lax.rem(core + step, layers) * q_block
                    xout[step - 1, j] = acc[
                        pl.ds(pl.multiple_of(theirs, q_block), q_block), pl.ds(j * tile, tile)
                    ].astype(jnp.bfloat16)
                    exchange(step, j).start()
        return carry

    lax.fori_loop(0, count, step, 0)

    def drain(at):
        sent = list(first[at])
        for group in groups[at]:
            for _, _, out in group:
                sent += out
        for i, route in enumerate(routes):
            total = sum(r == route for r, _ in sent)
            if total > 0:
                all_of_them = buf.at[pl.ds(0, total)]
                pltpu.make_async_remote_copy(
                    src_ref=all_of_them,
                    dst_ref=all_of_them,
                    send_sem=send_sem.at[i],
                    recv_sem=recv_sem.at[0],
                    device_id={"tok": partner["x"]},
                    device_id_type=MESH,
                ).wait_send()

    branch(role, 0, roles, drain)

    mine = pl.ds(pl.multiple_of(core * q_block, q_block), q_block)
    for j in range(tiles):
        at = pl.ds(j * tile, tile)
        for step in range(1, layers):
            exchange(step, j).wait_recv()
        result = acc[mine, at]
        for step in range(1, layers):
            result = result + xbuf[step - 1, j].astype(jnp.float32)
        out_ref[:, at] = result
    for j in range(tiles):
        for step in range(1, layers):
            exchange(step, j).wait_send()


def on_device(layers, toks, train_act, train_grad, test_act, test_grad, segment_ids):
    layer_count, train_rows, width = train_act.shape
    rows = test_act.shape[1]
    line = toks // 4
    first, log = route_blocks(line, layer_count)
    groups = [gather_groups(received) for received in log]
    tile = math.gcd(train_rows, 2048)
    tiles = train_rows // tile
    q_block = Q // layers
    ids = segment_ids.reshape(toks, 1, rows)
    dma = pltpu.SemaphoreType.DMA
    in_hbm = pl.BlockSpec(memory_space=pltpu.HBM)
    return pl.pallas_call(
        functools.partial(kernel, layers, line, first, groups),
        out_shape=pltpu.VMEM((q_block, train_rows), jnp.float32),
        in_specs=[in_hbm] * 5,
        out_specs=pl.BlockSpec(memory_space=pltpu.VMEM),
        scratch_shapes=[
            pltpu.VMEM((toks, 1, rows), jnp.int32),
            pltpu.VMEM((2 * rows, train_rows), jnp.bfloat16),
            pltpu.VMEM((2, layer_count, train_rows, width), jnp.bfloat16),
            pltpu.VMEM((toks * layer_count * 2, rows, width), jnp.bfloat16),
            pltpu.VMEM((Q, train_rows), jnp.float32),
            pltpu.VMEM((layers - 1, tiles, q_block, tile), jnp.bfloat16),
            pltpu.VMEM((layers - 1, tiles, q_block, tile), jnp.bfloat16),
            dma((2,)),
            dma((1,)),
            dma((max(len(g) for g in groups),)),
            dma((4,)),
            pltpu.SemaphoreType.REGULAR((3,)),
            dma((layers - 1, tiles)),
            dma((layers - 1, tiles)),
        ],
        compiler_params=pltpu.CompilerParams(
            collective_id=0, has_side_effects=True, vmem_limit_bytes=LIMIT
        ),
    )(train_act, train_grad, test_act, test_grad, ids)


def solution(mesh):
    placed = (
        P("layer", "tok", None),
        P("layer", "tok", None),
        P("layer", "tok", None),
        P("layer", "tok", None),
        P(),
    )
    body = functools.partial(on_device, mesh.shape["layer"], mesh.shape["tok"])
    return jax.shard_map(
        body, mesh=mesh, in_specs=placed, out_specs=P("layer", "tok"), check_vma=False
    )
```

```python
import functools
import heapq
import math

import jax
import jax.numpy as jnp
from jax import lax
from jax.experimental import pallas as pl
from jax.experimental.pallas import tpu as pltpu
from jax.sharding import PartitionSpec as P

Q = 128
MESH = pl.DeviceIdType.MESH
OWN, XSIDE, YSIDE, DIAG = range(4)
ACT, GRAD = range(2)

LIMIT = 60 * 1024 * 1024

CHUNK_TIME = 1.4
HOP_TIME = 1.7
POLL_TIME = 0.5
GROUP_TIME = 0.3
AHEAD_TIME = 0.5
LOAD_TIME = 3.0
UNIT_TIME = 1.0


def route_blocks(line, layers):
    reach = (2 + line) // 3
    even = line % 2 == 0
    free, events, log = {}, [], [[] for _ in range(line)]
    expected = {(at, "up"): 2 * layers * at for at in range(line)}
    expected |= {(at, "down"): 2 * layers * (line - 1 - at) for at in range(line)}
    held = {key: [] for key in expected}

    def flipped(at):
        return even and 2 * at > line - 1

    def send(time, at, route, chunk):
        start = max(free.get((at, route), 0.0), time)
        free[at, route] = start + CHUNK_TIME
        there = at + {"x": 0, "y": 0, "up": 1, "down": -1}[route]
        column, plane, which, layer = chunk
        seen = line - 1 - plane if flipped(there) else plane
        role = line - 1 - there if flipped(there) else there
        key = (round(start + CHUNK_TIME + HOP_TIME, 3), role, seen, column, layer, which, there)
        heapq.heappush(events, (key, chunk))

    def passes(at, chunk):
        column, plane, which, layer = chunk
        along = []
        if plane <= at < line - 1:
            along.append(("up", at + 1))
        if plane >= at > 0:
            along.append(("down", at - 1))
        if flipped(at):
            along.reverse()
        distance = abs(plane - at)
        far = distance > reach
        out = []
        if column == OWN:
            out += [(route, chunk) for route, _ in along]
            if plane != at:
                for route, _ in along:
                    expected[at, route] -= 1
                    if expected[at, route] == 0:
                        out += held[at, route]
                out.append(("y", (YSIDE, plane, which, layer)))
                late = far and layer == layers - 1
                if which == GRAD or not late:
                    out.append(("x", (XSIDE, plane, which, layer)))
                if which == GRAD and late:
                    out.append(("x", (XSIDE, plane, ACT, layer)))
        if column == DIAG:
            for route, to in along:
                if abs(plane - to) <= reach:
                    wait = expected[at, route] > 0
                    (held[at, route] if wait else out).append((route, chunk))
        if far or distance == 0:
            if column == YSIDE and which == ACT:
                out.append(("x", (DIAG, plane, which, layer)))
            if column == XSIDE and which == GRAD:
                out.append(("y", (DIAG, plane, which, layer)))
        return out

    first = []
    for at in range(line):
        mine = []
        for i in range(2 * layers):
            mine += passes(at, (OWN, at, i % 2, i // 2))
            mine.append(("x", (XSIDE, at, 1 - i // layers, i % layers)))
            mine.append(("y", (YSIDE, at, i // layers, i % layers)))
        for route, chunk in mine:
            send(0.0, at, route, chunk)
        first.append(mine)
    while events:
        (time, *_, at), chunk = heapq.heappop(events)
        out = passes(at, chunk)
        for route, sent in out:
            send(time + POLL_TIME, at, route, sent)
        log[at].append((time, chunk, out))
    return first, log


def gather_groups(log):
    groups, opened = [], 0.0
    for time, chunk, out in log:
        if not groups or time > opened + GROUP_TIME:
            groups.append([])
            opened = time
        groups[-1].append((time, chunk, out))
    return groups


def plan_steps(at, layers, groups):
    ready = {(OWN, at, layer): 0.0 for layer in range(layers)}
    for group in groups:
        for _, (column, plane, _, layer), _ in group:
            ready[column, plane, layer] = group[-1][0]
    blocks = sorted(
        {key[:2] for key in ready}, key=lambda b: [ready[(*b, l)] for l in range(layers)][::-1]
    )
    units = []
    for one, two in zip(blocks[::2], blocks[1::2]):
        for layer in range(layers):
            units.append((max(ready[(*one, layer)], ready[(*two, layer)]), one, two, layer))
    units.sort(key=lambda unit: unit[0])
    steps, now, i = [], LOAD_TIME, 0
    for k, (time, one, two, layer) in enumerate(units):
        now = max(now, time)
        moves = []
        while i < len(groups) and (
            groups[i][-1][0] <= now + AHEAD_TIME or k == len(units) - 1
        ):
            now = max(now, groups[i][-1][0])
            moves.append(i)
            i += 1
        steps.append((moves, one, two, layer))
        now += UNIT_TIME
    return steps


def branch(value, low, high, leaf):
    if high - low == 1:
        leaf(low)
        return
    middle = (low + high) // 2
    pl.when(value < middle)(lambda: branch(value, low, middle, leaf))
    pl.when(value >= middle)(lambda: branch(value, middle, high, leaf))


def pick(index, values):
    result = jnp.int32(values[-1])
    for i, value in enumerate(values[:-1]):
        result = jnp.where(index == i, jnp.int32(value), result)
    return result


def kernel(
    layers,
    line,
    first,
    groups,
    train_a,
    train_g,
    test_a,
    test_g,
    ids_hbm,
    out_ref,
    ids_ref,
    prod,
    train,
    buf,
    acc,
    xbuf,
    xout,
    train_sem,
    own_sem,
    recv_sem,
    send_sem,
    ready_sem,
    xs_sem,
    xr_sem,
):
    me = lax.axis_index("tok")
    core = lax.axis_index("layer")
    z = me // 4
    y = (me // 2) % 2
    x = me % 2
    columns = (
        y * 2 + x,
        y * 2 + (1 - x),
        (1 - y) * 2 + x,
        (1 - y) * 2 + (1 - x),
    )
    _, layer_count, train_rows, _ = train.shape
    _, rows, width = buf.shape
    q_block = Q // layers
    has_up = z < line - 1
    has_down = z > 0

    roles = line // 2 if line % 2 == 0 else line
    flip = (z >= roles).astype(jnp.int32)
    role = jnp.where(flip == 1, line - 1 - z, z)
    sign = 1 - 2 * flip
    partner = {
        "x": z * 4 + columns[XSIDE],
        "y": z * 4 + columns[YSIDE],
        "up": me + 4 * sign,
        "down": me - 4 * sign,
    }
    routes = tuple(partner)
    group_of = [
        {chunk: i for i, group in enumerate(groups[at]) for _, chunk, _ in group}
        for at in range(roles)
    ]

    def group_there(at, route, chunk):
        column, plane, which, layer = chunk
        there = at + {"x": 0, "y": 0, "up": 1, "down": -1}[route]
        if there >= roles:
            there, plane = line - 1 - there, line - 1 - plane
        return group_of[there][column, plane, which, layer]

    across = {
        "x": (XSIDE, OWN, DIAG, YSIDE),
        "y": (YSIDE, DIAG, OWN, XSIDE),
        "up": (OWN, XSIDE, YSIDE, DIAG),
        "down": (OWN, XSIDE, YSIDE, DIAG),
    }

    def place(column, plane):
        return jnp.where(flip == 1, line - 1 - plane, plane) * 4 + columns[column]

    def slot(column, plane, which, layer):
        return (place(column, plane) * layer_count + layer) * 2 + which


    def own_copy(which, layer):
        src = (test_a, test_g)[which]
        return pltpu.make_async_copy(
            src.at[layer],
            buf.at[(me * layer_count + layer) * 2 + which],
            own_sem.at[0],
        )

    for which in range(2):
        for layer in range(layer_count):
            own_copy(which, layer).start()
    ids_copy = pltpu.make_async_copy(ids_hbm, ids_ref, train_sem.at[1])
    ids_copy.start()

    lower = {"x": x == 1, "y": y == 1, "up": flip == 1, "down": flip == 0}
    axis = {"x": 0, "y": 1, "up": 2, "down": 2}
    barrier = pltpu.get_barrier_semaphore()

    def greet(where, semaphore=barrier):
        pl.semaphore_signal(semaphore, inc=1, device_id=where, device_id_type=MESH)

    pl.when(x == 0)(lambda: greet({"tok": partner["x"]}))
    pl.when(y == 0)(lambda: greet({"tok": partner["y"]}))
    pl.when(has_up)(lambda: greet({"tok": me + 4}))
    for other in range(layers):
        pl.when(other > core)(functools.partial(greet, {"layer": other}))
    before = core + x + y + has_down.astype(jnp.int32)
    pl.when(before > 0)(lambda: pl.semaphore_wait(barrier, before))
    pl.when(x == 1)(lambda: greet({"tok": partner["x"]}, ready_sem.at[0]))
    pl.when(y == 1)(lambda: greet({"tok": partner["y"]}, ready_sem.at[1]))
    pl.when(has_down)(lambda: greet({"tok": me - 4}, ready_sem.at[2]))
    for other in range(layers):
        pl.when(other < core)(functools.partial(greet, {"layer": other}, ready_sem.at[3]))

    def copy(at, route, chunk, src=None):
        column, plane, which, layer = chunk
        here = slot(across[route][column], plane, which, layer)
        return pltpu.make_async_remote_copy(
            src_ref=buf.at[here] if src is None else src,
            dst_ref=buf.at[here],
            send_sem=send_sem.at[routes.index(route)],
            recv_sem=recv_sem.at[group_there(at, route, chunk)],
            device_id={"tok": partner[route]},
            device_id_type=MESH,
        )

    def arrived(index, size):
        pltpu.make_async_remote_copy(
            src_ref=buf.at[pl.ds(0, size)],
            dst_ref=buf.at[pl.ds(0, size)],
            send_sem=send_sem.at[0],
            recv_sem=recv_sem.at[index],
            device_id={"tok": partner["x"]},
            device_id_type=MESH,
        ).wait_recv()

    steps = [plan_steps(at, layer_count, groups[at]) for at in range(roles)]
    count = len(steps[0])

    def send_own(at):
        def send(route):
            for own_route, chunk in first[at]:
                if own_route == route:
                    src = (test_a, test_g)[chunk[2]].at[chunk[3]]
                    copy(at, route, chunk, src).start()

        def answered(route):
            pl.semaphore_wait(ready_sem.at[axis[route]], 1)
            send(route)

        used = sorted({route for route, _ in first[at]}, key=routes.index)
        for route in used:
            pl.when(lower[route])(functools.partial(send, route))
        for route in used:
            pl.when(jnp.logical_not(lower[route]))(functools.partial(answered, route))

    branch(role, 0, roles, send_own)

    for which, src in enumerate((train_a, train_g)):
        pltpu.make_async_copy(src, train.at[which], train_sem.at[0]).start()

    after = layers - 1 - core
    pl.when(after > 0)(lambda: pl.semaphore_wait(ready_sem.at[3], after))
    acc[...] = jnp.zeros_like(acc)
    _, tiles, _, tile = xbuf.shape
    labels = lax.broadcasted_iota(jnp.int32, (Q, rows), 0)
    nt = (((1,), (1,)), ((), ()))

    def exchange(step, j):
        to = lax.rem(core + step, layers)
        return pltpu.make_async_remote_copy(
            src_ref=xout.at[step - 1, j],
            dst_ref=xbuf.at[step - 1, j],
            send_sem=xs_sem.at[step - 1, j],
            recv_sem=xr_sem.at[step - 1, j],
            device_id={"layer": to},
            device_id_type=MESH,
        )

    ids_copy.wait()
    own_all = buf.at[pl.ds(me * layer_count * 2, layer_count * 2)]
    pltpu.make_async_copy(own_all, own_all, own_sem.at[0]).wait()
    pltpu.make_async_copy(train, train, train_sem.at[0]).wait()

    def relay(k, at):
        for index in steps[at][k][0]:
            group = groups[at][index]
            arrived(index, len(group))
            for _, _, out in group:
                for route, sent in out:
                    copy(at, route, sent).start()

    base = line * 4
    packed = [
        (
            ((one[1] * 4 + one[0]) * base + two[1] * 4 + two[0]) * layer_count + layer
        )
        for at in range(roles)
        for _, one, two, layer in steps[at]
    ]

    def position(code):
        plane, column = code // 4, code % 4
        plane = jnp.where(flip == 1, line - 1 - plane, plane)
        return plane * 4 + pick(column, columns)

    def step(k, carry):
        code = pick(role * count + k, packed)
        layer = code % layer_count
        one = position(code // layer_count // base)
        two = position((code // layer_count) % base)
        select = jnp.concatenate(
            [
                jnp.where(ids_ref[b] == labels, 1.0, 0.0).astype(jnp.bfloat16)
                for b in (one, two)
            ],
            axis=1,
        )

        branch(k, 0, count, lambda k0: branch(role, 0, roles, functools.partial(relay, k0)))

        def held(which):
            return jnp.concatenate(
                [buf[(b * layer_count + layer) * 2 + which] for b in (one, two)], axis=0
            )

        a_held, g_held = held(ACT), held(GRAD)

        a_gram = lax.dot_general(a_held, train[ACT, layer], nt, preferred_element_type=jnp.float32)
        g_gram = lax.dot_general(g_held, train[GRAD, layer], nt, preferred_element_type=jnp.float32)
        prod[...] = (a_gram * g_gram).astype(jnp.bfloat16)

        acc[...] += jnp.dot(select, prod[...], preferred_element_type=jnp.float32)

        @pl.when(k == count - 1)
        def _():
            for j in range(tiles):
                for step in range(1, layers):
                    theirs = lax.rem(core + step, layers) * q_block
                    xout[step - 1, j] = acc[
                        pl.ds(pl.multiple_of(theirs, q_block), q_block), pl.ds(j * tile, tile)
                    ].astype(jnp.bfloat16)
                    exchange(step, j).start()
        return carry

    lax.fori_loop(0, count, step, 0)

    def drain(at):
        sent = list(first[at])
        for group in groups[at]:
            for _, _, out in group:
                sent += out
        for i, route in enumerate(routes):
            total = sum(r == route for r, _ in sent)
            if total > 0:
                all_of_them = buf.at[pl.ds(0, total)]
                pltpu.make_async_remote_copy(
                    src_ref=all_of_them,
                    dst_ref=all_of_them,
                    send_sem=send_sem.at[i],
                    recv_sem=recv_sem.at[0],
                    device_id={"tok": partner["x"]},
                    device_id_type=MESH,
                ).wait_send()

    branch(role, 0, roles, drain)

    mine = pl.ds(pl.multiple_of(core * q_block, q_block), q_block)
    for j in range(tiles):
        at = pl.ds(j * tile, tile)
        for step in range(1, layers):
            exchange(step, j).wait_recv()
        result = acc[mine, at]
        for step in range(1, layers):
            result = result + xbuf[step - 1, j].astype(jnp.float32)
        out_ref[:, at] = result
    for j in range(tiles):
        for step in range(1, layers):
            exchange(step, j).wait_send()


def on_device(layers, toks, train_act, train_grad, test_act, test_grad, segment_ids):
    layer_count, train_rows, width = train_act.shape
    rows = test_act.shape[1]
    line = toks // 4
    first, log = route_blocks(line, layer_count)
    groups = [gather_groups(received) for received in log]
    tile = math.gcd(train_rows, 2048)
    tiles = train_rows // tile
    q_block = Q // layers
    ids = segment_ids.reshape(toks, 1, rows)
    dma = pltpu.SemaphoreType.DMA
    in_hbm = pl.BlockSpec(memory_space=pltpu.HBM)
    return pl.pallas_call(
        functools.partial(kernel, layers, line, first, groups),
        out_shape=pltpu.VMEM((q_block, train_rows), jnp.float32),
        in_specs=[in_hbm] * 5,
        out_specs=pl.BlockSpec(memory_space=pltpu.VMEM),
        scratch_shapes=[
            pltpu.VMEM((toks, 1, rows), jnp.int32),
            pltpu.VMEM((2 * rows, train_rows), jnp.bfloat16),
            pltpu.VMEM((2, layer_count, train_rows, width), jnp.bfloat16),
            pltpu.VMEM((toks * layer_count * 2, rows, width), jnp.bfloat16),
            pltpu.VMEM((Q, train_rows), jnp.float32),
            pltpu.VMEM((layers - 1, tiles, q_block, tile), jnp.bfloat16),
            pltpu.VMEM((layers - 1, tiles, q_block, tile), jnp.bfloat16),
            dma((2,)),
            dma((1,)),
            dma((max(len(g) for g in groups),)),
            dma((4,)),
            pltpu.SemaphoreType.REGULAR((4,)),
            dma((layers - 1, tiles)),
            dma((layers - 1, tiles)),
        ],
        compiler_params=pltpu.CompilerParams(
            collective_id=0, has_side_effects=True, vmem_limit_bytes=LIMIT
        ),
    )(train_act, train_grad, test_act, test_grad, ids)


def solution(mesh):
    placed = (
        P("layer", "tok", None),
        P("layer", "tok", None),
        P("layer", "tok", None),
        P("layer", "tok", None),
        P(),
    )
    body = functools.partial(on_device, mesh.shape["layer"], mesh.shape["tok"])
    return jax.shard_map(
        body, mesh=mesh, in_specs=placed, out_specs=P("layer", "tok"), check_vma=False
    )
```

```python
import functools
import heapq
import math

import jax
import jax.numpy as jnp
from jax import lax
from jax.experimental import pallas as pl
from jax.experimental.pallas import tpu as pltpu
from jax.sharding import PartitionSpec as P

Q = 128
MESH = pl.DeviceIdType.MESH
OWN, XSIDE, YSIDE, DIAG = range(4)
ACT, GRAD = range(2)

LIMIT = 60 * 1024 * 1024

CHUNK_TIME = 1.4
HOP_TIME = 1.7
POLL_TIME = 0.5
GROUP_TIME = 0.3
AHEAD_TIME = 0.5
LOAD_TIME = 3.0
UNIT_TIME = 1.0


def route_blocks(line, layers):
    reach = (2 + line) // 3
    even = line % 2 == 0
    free, events, log = {}, [], [[] for _ in range(line)]
    expected = {(at, "up"): 2 * layers * at for at in range(line)}
    expected |= {(at, "down"): 2 * layers * (line - 1 - at) for at in range(line)}
    held = {key: [] for key in expected}

    def flipped(at):
        return even and 2 * at > line - 1

    def send(time, at, route, chunk):
        start = max(free.get((at, route), 0.0), time)
        free[at, route] = start + CHUNK_TIME
        there = at + {"x": 0, "y": 0, "up": 1, "down": -1}[route]
        column, plane, which, layer = chunk
        seen = line - 1 - plane if flipped(there) else plane
        role = line - 1 - there if flipped(there) else there
        key = (round(start + CHUNK_TIME + HOP_TIME, 3), role, seen, column, layer, which, there)
        heapq.heappush(events, (key, chunk))

    def passes(at, chunk):
        column, plane, which, layer = chunk
        along = []
        if plane <= at < line - 1:
            along.append(("up", at + 1))
        if plane >= at > 0:
            along.append(("down", at - 1))
        if flipped(at):
            along.reverse()
        distance = abs(plane - at)
        far = distance > reach
        out = []
        if column == OWN:
            out += [(route, chunk) for route, _ in along]
            if plane != at:
                for route, _ in along:
                    expected[at, route] -= 1
                    if expected[at, route] == 0:
                        out += held[at, route]
                out.append(("y", (YSIDE, plane, which, layer)))
                late = far and layer == layers - 1
                if which == GRAD or not late:
                    out.append(("x", (XSIDE, plane, which, layer)))
                if which == GRAD and late:
                    out.append(("x", (XSIDE, plane, ACT, layer)))
        if column == DIAG:
            for route, to in along:
                if abs(plane - to) <= reach:
                    wait = expected[at, route] > 0
                    (held[at, route] if wait else out).append((route, chunk))
        if far or distance == 0:
            if column == YSIDE and which == ACT:
                out.append(("x", (DIAG, plane, which, layer)))
            if column == XSIDE and which == GRAD:
                out.append(("y", (DIAG, plane, which, layer)))
        return out

    first = []
    for at in range(line):
        mine = []
        for i in range(2 * layers):
            mine += passes(at, (OWN, at, i % 2, i // 2))
            mine.append(("x", (XSIDE, at, 1 - i // layers, i % layers)))
            mine.append(("y", (YSIDE, at, i // layers, i % layers)))
        for route, chunk in mine:
            send(0.0, at, route, chunk)
        first.append(mine)
    while events:
        (time, *_, at), chunk = heapq.heappop(events)
        out = passes(at, chunk)
        for route, sent in out:
            send(time + POLL_TIME, at, route, sent)
        log[at].append((time, chunk, out))
    return first, log


def gather_groups(log):
    groups, opened = [], 0.0
    for time, chunk, out in log:
        if not groups or time > opened + GROUP_TIME:
            groups.append([])
            opened = time
        groups[-1].append((time, chunk, out))
    return groups


def plan_steps(at, layers, groups):
    ready = {(OWN, at, layer): 0.0 for layer in range(layers)}
    for group in groups:
        for _, (column, plane, _, layer), _ in group:
            ready[column, plane, layer] = group[-1][0]
    blocks = sorted(
        {key[:2] for key in ready}, key=lambda b: [ready[(*b, l)] for l in range(layers)][::-1]
    )
    units = []
    for one, two in zip(blocks[::2], blocks[1::2]):
        for layer in range(layers):
            units.append((max(ready[(*one, layer)], ready[(*two, layer)]), one, two, layer))
    units.sort(key=lambda unit: unit[0])
    steps, now, i = [], LOAD_TIME, 0
    for k, (time, one, two, layer) in enumerate(units):
        now = max(now, time)
        moves = []
        while i < len(groups) and (
            groups[i][-1][0] <= now + AHEAD_TIME or k == len(units) - 1
        ):
            now = max(now, groups[i][-1][0])
            moves.append(i)
            i += 1
        steps.append((moves, one, two, layer))
        now += UNIT_TIME
    return steps


def branch(value, low, high, leaf):
    if high - low == 1:
        leaf(low)
        return
    middle = (low + high) // 2
    pl.when(value < middle)(lambda: branch(value, low, middle, leaf))
    pl.when(value >= middle)(lambda: branch(value, middle, high, leaf))


def pick(index, values):
    result = jnp.int32(values[-1])
    for i, value in enumerate(values[:-1]):
        result = jnp.where(index == i, jnp.int32(value), result)
    return result


def kernel(
    layers,
    line,
    first,
    groups,
    train_a,
    train_g,
    test_a,
    test_g,
    ids_hbm,
    out_ref,
    ids_ref,
    prod,
    train,
    buf,
    acc,
    xbuf,
    xout,
    train_sem,
    own_sem,
    recv_sem,
    send_sem,
    ready_sem,
    xs_sem,
    xr_sem,
):
    me = lax.axis_index("tok")
    core = lax.axis_index("layer")
    z = me // 4
    y = (me // 2) % 2
    x = me % 2
    columns = (
        y * 2 + x,
        y * 2 + (1 - x),
        (1 - y) * 2 + x,
        (1 - y) * 2 + (1 - x),
    )
    _, layer_count, train_rows, _ = train.shape
    _, rows, width = buf.shape
    q_block = Q // layers
    has_up = z < line - 1
    has_down = z > 0

    roles = line // 2 if line % 2 == 0 else line
    flip = (z >= roles).astype(jnp.int32)
    role = jnp.where(flip == 1, line - 1 - z, z)
    sign = 1 - 2 * flip
    partner = {
        "x": z * 4 + columns[XSIDE],
        "y": z * 4 + columns[YSIDE],
        "up": me + 4 * sign,
        "down": me - 4 * sign,
    }
    routes = tuple(partner)
    group_of = [
        {chunk: i for i, group in enumerate(groups[at]) for _, chunk, _ in group}
        for at in range(roles)
    ]

    def group_there(at, route, chunk):
        column, plane, which, layer = chunk
        there = at + {"x": 0, "y": 0, "up": 1, "down": -1}[route]
        if there >= roles:
            there, plane = line - 1 - there, line - 1 - plane
        return group_of[there][column, plane, which, layer]

    across = {
        "x": (XSIDE, OWN, DIAG, YSIDE),
        "y": (YSIDE, DIAG, OWN, XSIDE),
        "up": (OWN, XSIDE, YSIDE, DIAG),
        "down": (OWN, XSIDE, YSIDE, DIAG),
    }

    def place(column, plane):
        return jnp.where(flip == 1, line - 1 - plane, plane) * 4 + columns[column]

    def slot(column, plane, which, layer):
        return (place(column, plane) * layer_count + layer) * 2 + which


    def own_copy(which, layer):
        src = (test_a, test_g)[which]
        return pltpu.make_async_copy(
            src.at[layer],
            buf.at[(me * layer_count + layer) * 2 + which],
            own_sem.at[0],
        )

    for which in range(2):
        for layer in range(layer_count):
            own_copy(which, layer).start()
    ids_copy = pltpu.make_async_copy(ids_hbm, ids_ref, train_sem.at[1])
    ids_copy.start()

    lower = {"x": x == 1, "y": y == 1, "up": flip == 1, "down": flip == 0}
    axis = {"x": 0, "y": 1, "up": 2, "down": 2}
    barrier = pltpu.get_barrier_semaphore()

    def greet(where, semaphore=barrier):
        pl.semaphore_signal(semaphore, inc=1, device_id=where, device_id_type=MESH)

    pl.when(x == 0)(lambda: greet({"tok": partner["x"]}))
    pl.when(y == 0)(lambda: greet({"tok": partner["y"]}))
    pl.when(has_up)(lambda: greet({"tok": me + 4}))
    for other in range(layers):
        pl.when(other > core)(functools.partial(greet, {"layer": other}))
    before = core + x + y + has_down.astype(jnp.int32)
    pl.when(before > 0)(lambda: pl.semaphore_wait(barrier, before))
    pl.when(x == 1)(lambda: greet({"tok": partner["x"]}, ready_sem.at[0]))
    pl.when(y == 1)(lambda: greet({"tok": partner["y"]}, ready_sem.at[1]))
    pl.when(has_down)(lambda: greet({"tok": me - 4}, ready_sem.at[2]))
    for other in range(layers):
        pl.when(other < core)(functools.partial(greet, {"layer": other}, ready_sem.at[3]))

    def copy(at, route, chunk, src=None):
        column, plane, which, layer = chunk
        here = slot(across[route][column], plane, which, layer)
        return pltpu.make_async_remote_copy(
            src_ref=buf.at[here] if src is None else src,
            dst_ref=buf.at[here],
            send_sem=send_sem.at[axis[route] // 2],
            recv_sem=recv_sem.at[group_there(at, route, chunk)],
            device_id={"tok": partner[route]},
            device_id_type=MESH,
        )

    def arrived(index, size):
        pltpu.make_async_remote_copy(
            src_ref=buf.at[pl.ds(0, size)],
            dst_ref=buf.at[pl.ds(0, size)],
            send_sem=send_sem.at[0],
            recv_sem=recv_sem.at[index],
            device_id={"tok": partner["x"]},
            device_id_type=MESH,
        ).wait_recv()

    steps = [plan_steps(at, layer_count, groups[at]) for at in range(roles)]
    count = len(steps[0])

    def send_own(at):
        def send(route):
            for own_route, chunk in first[at]:
                if own_route == route:
                    src = (test_a, test_g)[chunk[2]].at[chunk[3]]
                    copy(at, route, chunk, src).start()

        def answered(route):
            pl.semaphore_wait(ready_sem.at[axis[route]], 1)
            send(route)

        used = sorted({route for route, _ in first[at]}, key=routes.index)
        for route in used:
            pl.when(lower[route])(functools.partial(send, route))
        for route in used:
            pl.when(jnp.logical_not(lower[route]))(functools.partial(answered, route))

    branch(role, 0, roles, send_own)

    for which, src in enumerate((train_a, train_g)):
        pltpu.make_async_copy(src, train.at[which], train_sem.at[0]).start()

    after = layers - 1 - core
    pl.when(after > 0)(lambda: pl.semaphore_wait(ready_sem.at[3], after))
    acc[...] = jnp.zeros_like(acc)
    _, tiles, _, tile = xbuf.shape
    labels = lax.broadcasted_iota(jnp.int32, (Q, rows), 0)
    nt = (((1,), (1,)), ((), ()))

    def exchange(step, j):
        to = lax.rem(core + step, layers)
        return pltpu.make_async_remote_copy(
            src_ref=xout.at[step - 1, j],
            dst_ref=xbuf.at[step - 1, j],
            send_sem=xs_sem.at[step - 1, j],
            recv_sem=xr_sem.at[step - 1, j],
            device_id={"layer": to},
            device_id_type=MESH,
        )

    ids_copy.wait()
    own_all = buf.at[pl.ds(me * layer_count * 2, layer_count * 2)]
    pltpu.make_async_copy(own_all, own_all, own_sem.at[0]).wait()
    pltpu.make_async_copy(train, train, train_sem.at[0]).wait()

    def relay(k, at):
        for index in steps[at][k][0]:
            group = groups[at][index]
            arrived(index, len(group))
            for _, _, out in group:
                for route, sent in out:
                    copy(at, route, sent).start()

    base = line * 4
    packed = [
        (
            ((one[1] * 4 + one[0]) * base + two[1] * 4 + two[0]) * layer_count + layer
        )
        for at in range(roles)
        for _, one, two, layer in steps[at]
    ]

    def position(code):
        plane, column = code // 4, code % 4
        plane = jnp.where(flip == 1, line - 1 - plane, plane)
        return plane * 4 + pick(column, columns)

    def step(k, carry):
        code = pick(role * count + k, packed)
        layer = code % layer_count
        one = position(code // layer_count // base)
        two = position((code // layer_count) % base)
        select = jnp.concatenate(
            [
                jnp.where(ids_ref[b] == labels, 1.0, 0.0).astype(jnp.bfloat16)
                for b in (one, two)
            ],
            axis=1,
        )

        branch(k, 0, count, lambda k0: branch(role, 0, roles, functools.partial(relay, k0)))

        def held(which):
            return jnp.concatenate(
                [buf[(b * layer_count + layer) * 2 + which] for b in (one, two)], axis=0
            )

        a_held, g_held = held(ACT), held(GRAD)

        a_gram = lax.dot_general(a_held, train[ACT, layer], nt, preferred_element_type=jnp.float32)
        g_gram = lax.dot_general(g_held, train[GRAD, layer], nt, preferred_element_type=jnp.float32)
        prod[...] = (a_gram * g_gram).astype(jnp.bfloat16)

        acc[...] += jnp.dot(select, prod[...], preferred_element_type=jnp.float32)

        @pl.when(k == count - 1)
        def _():
            for j in range(tiles):
                for step in range(1, layers):
                    theirs = lax.rem(core + step, layers) * q_block
                    xout[step - 1, j] = acc[
                        pl.ds(pl.multiple_of(theirs, q_block), q_block), pl.ds(j * tile, tile)
                    ].astype(jnp.bfloat16)
                    exchange(step, j).start()
        return carry

    lax.fori_loop(0, count, step, 0)

    def drain(at):
        sent = list(first[at])
        for group in groups[at]:
            for _, _, out in group:
                sent += out
        for i in range(2):
            total = sum(axis[route] // 2 == i for route, _ in sent)
            if total > 0:
                all_of_them = buf.at[pl.ds(0, total)]
                pltpu.make_async_remote_copy(
                    src_ref=all_of_them,
                    dst_ref=all_of_them,
                    send_sem=send_sem.at[i],
                    recv_sem=recv_sem.at[0],
                    device_id={"tok": partner["x"]},
                    device_id_type=MESH,
                ).wait_send()

    branch(role, 0, roles, drain)

    mine = pl.ds(pl.multiple_of(core * q_block, q_block), q_block)
    for j in range(tiles):
        at = pl.ds(j * tile, tile)
        for step in range(1, layers):
            exchange(step, j).wait_recv()
        result = acc[mine, at]
        for step in range(1, layers):
            result = result + xbuf[step - 1, j].astype(jnp.float32)
        out_ref[:, at] = result
    for j in range(tiles):
        for step in range(1, layers):
            exchange(step, j).wait_send()


def on_device(layers, toks, train_act, train_grad, test_act, test_grad, segment_ids):
    layer_count, train_rows, width = train_act.shape
    rows = test_act.shape[1]
    line = toks // 4
    first, log = route_blocks(line, layer_count)
    groups = [gather_groups(received) for received in log]
    tile = math.gcd(train_rows, 2048)
    tiles = train_rows // tile
    q_block = Q // layers
    ids = segment_ids.reshape(toks, 1, rows)
    dma = pltpu.SemaphoreType.DMA
    in_hbm = pl.BlockSpec(memory_space=pltpu.HBM)
    return pl.pallas_call(
        functools.partial(kernel, layers, line, first, groups),
        out_shape=pltpu.VMEM((q_block, train_rows), jnp.float32),
        in_specs=[in_hbm] * 5,
        out_specs=pl.BlockSpec(memory_space=pltpu.VMEM),
        scratch_shapes=[
            pltpu.VMEM((toks, 1, rows), jnp.int32),
            pltpu.VMEM((2 * rows, train_rows), jnp.bfloat16),
            pltpu.VMEM((2, layer_count, train_rows, width), jnp.bfloat16),
            pltpu.VMEM((toks * layer_count * 2, rows, width), jnp.bfloat16),
            pltpu.VMEM((Q, train_rows), jnp.float32),
            pltpu.VMEM((layers - 1, tiles, q_block, tile), jnp.bfloat16),
            pltpu.VMEM((layers - 1, tiles, q_block, tile), jnp.bfloat16),
            dma((2,)),
            dma((1,)),
            dma((max(len(g) for g in groups),)),
            dma((2,)),
            pltpu.SemaphoreType.REGULAR((4,)),
            dma((layers - 1, tiles)),
            dma((layers - 1, tiles)),
        ],
        compiler_params=pltpu.CompilerParams(
            collective_id=0, has_side_effects=True, vmem_limit_bytes=LIMIT
        ),
    )(train_act, train_grad, test_act, test_grad, ids)


def solution(mesh):
    placed = (
        P("layer", "tok", None),
        P("layer", "tok", None),
        P("layer", "tok", None),
        P("layer", "tok", None),
        P(),
    )
    body = functools.partial(on_device, mesh.shape["layer"], mesh.shape["tok"])
    return jax.shard_map(
        body, mesh=mesh, in_specs=placed, out_specs=P("layer", "tok"), check_vma=False
    )
```

```python
import functools
import heapq
import math

import jax
import jax.numpy as jnp
from jax import lax
from jax.experimental import pallas as pl
from jax.experimental.pallas import tpu as pltpu
from jax.sharding import PartitionSpec as P

Q = 128
MESH = pl.DeviceIdType.MESH
OWN, XSIDE, YSIDE, DIAG = range(4)
ACT, GRAD = range(2)

LIMIT = 60 * 1024 * 1024

CHUNK_TIME = 1.4
HOP_TIME = 1.7
POLL_TIME = 0.5
GROUP_TIME = 0.3
AHEAD_TIME = 0.5
LOAD_TIME = 3.0
UNIT_TIME = 1.0


def route_blocks(line, layers):
    reach = (2 + line) // 3
    even = line % 2 == 0
    free, events, log = {}, [], [[] for _ in range(line)]
    expected = {(at, "up"): 2 * layers * at for at in range(line)}
    expected |= {(at, "down"): 2 * layers * (line - 1 - at) for at in range(line)}
    held = {key: [] for key in expected}

    def flipped(at):
        return even and 2 * at > line - 1

    def send(time, at, route, chunk):
        start = max(free.get((at, route), 0.0), time)
        free[at, route] = start + CHUNK_TIME
        there = at + {"x": 0, "y": 0, "up": 1, "down": -1}[route]
        column, plane, which, layer = chunk
        seen = line - 1 - plane if flipped(there) else plane
        role = line - 1 - there if flipped(there) else there
        key = (round(start + CHUNK_TIME + HOP_TIME, 3), role, seen, column, layer, which, there)
        heapq.heappush(events, (key, chunk))

    def passes(at, chunk):
        column, plane, which, layer = chunk
        along = []
        if plane <= at < line - 1:
            along.append(("up", at + 1))
        if plane >= at > 0:
            along.append(("down", at - 1))
        if flipped(at):
            along.reverse()
        distance = abs(plane - at)
        far = distance > reach
        out = []
        if column == OWN:
            out += [(route, chunk) for route, _ in along]
            if plane != at:
                for route, _ in along:
                    expected[at, route] -= 1
                    if expected[at, route] == 0:
                        out += held[at, route]
                out.append(("y", (YSIDE, plane, which, layer)))
                late = far and layer == layers - 1
                if which == GRAD or not late:
                    out.append(("x", (XSIDE, plane, which, layer)))
                if which == GRAD and late:
                    out.append(("x", (XSIDE, plane, ACT, layer)))
        if column == DIAG:
            for route, to in along:
                if abs(plane - to) <= reach:
                    wait = expected[at, route] > 0
                    (held[at, route] if wait else out).append((route, chunk))
        if far or distance == 0:
            if column == YSIDE and which == ACT:
                out.append(("x", (DIAG, plane, which, layer)))
            if column == XSIDE and which == GRAD:
                out.append(("y", (DIAG, plane, which, layer)))
        return out

    first = []
    for at in range(line):
        mine = []
        for i in range(2 * layers):
            mine += passes(at, (OWN, at, i % 2, i // 2))
            mine.append(("x", (XSIDE, at, 1 - i // layers, i % layers)))
            mine.append(("y", (YSIDE, at, i // layers, i % layers)))
        for route, chunk in mine:
            send(0.0, at, route, chunk)
        first.append(mine)
    while events:
        (time, *_, at), chunk = heapq.heappop(events)
        out = passes(at, chunk)
        for route, sent in out:
            send(time + POLL_TIME, at, route, sent)
        log[at].append((time, chunk, out))
    return first, log


def gather_groups(log):
    groups, opened = [], 0.0
    for time, chunk, out in log:
        if not groups or time > opened + GROUP_TIME:
            groups.append([])
            opened = time
        groups[-1].append((time, chunk, out))
    return groups


def plan_steps(at, layers, groups):
    ready = {(OWN, at, layer): 0.0 for layer in range(layers)}
    for group in groups:
        for _, (column, plane, _, layer), _ in group:
            ready[column, plane, layer] = group[-1][0]
    blocks = sorted(
        {key[:2] for key in ready}, key=lambda b: [ready[(*b, l)] for l in range(layers)][::-1]
    )
    units = []
    for one, two in zip(blocks[::2], blocks[1::2]):
        for layer in range(layers):
            units.append((max(ready[(*one, layer)], ready[(*two, layer)]), one, two, layer))
    units.sort(key=lambda unit: unit[0])
    steps, now, i = [], LOAD_TIME, 0
    for k, (time, one, two, layer) in enumerate(units):
        now = max(now, time)
        moves = []
        while i < len(groups) and (
            groups[i][-1][0] <= now + AHEAD_TIME or k == len(units) - 1
        ):
            now = max(now, groups[i][-1][0])
            moves.append(i)
            i += 1
        steps.append((moves, one, two, layer))
        now += UNIT_TIME
    return steps


def branch(value, low, high, leaf):
    if high - low == 1:
        leaf(low)
        return
    middle = (low + high) // 2
    pl.when(value < middle)(lambda: branch(value, low, middle, leaf))
    pl.when(value >= middle)(lambda: branch(value, middle, high, leaf))


def pick(index, values):
    result = jnp.int32(values[-1])
    for i, value in enumerate(values[:-1]):
        result = jnp.where(index == i, jnp.int32(value), result)
    return result


def kernel(
    layers,
    line,
    first,
    groups,
    train_a,
    train_g,
    test_a,
    test_g,
    ids_hbm,
    out_ref,
    ids_ref,
    prod,
    train,
    buf,
    acc,
    xbuf,
    xout,
    train_sem,
    own_sem,
    recv_sem,
    send_sem,
    ready_sem,
    xs_sem,
    xr_sem,
):
    me = lax.axis_index("tok")
    core = lax.axis_index("layer")
    z = me // 4
    y = (me // 2) % 2
    x = me % 2
    columns = (
        y * 2 + x,
        y * 2 + (1 - x),
        (1 - y) * 2 + x,
        (1 - y) * 2 + (1 - x),
    )
    _, layer_count, train_rows, _ = train.shape
    _, rows, width = buf.shape
    q_block = Q // layers
    has_up = z < line - 1
    has_down = z > 0

    roles = line // 2 if line % 2 == 0 else line
    flip = (z >= roles).astype(jnp.int32)
    role = jnp.where(flip == 1, line - 1 - z, z)
    sign = 1 - 2 * flip
    partner = {
        "x": z * 4 + columns[XSIDE],
        "y": z * 4 + columns[YSIDE],
        "up": me + 4 * sign,
        "down": me - 4 * sign,
    }
    routes = tuple(partner)
    group_of = [
        {chunk: i for i, group in enumerate(groups[at]) for _, chunk, _ in group}
        for at in range(roles)
    ]

    def group_there(at, route, chunk):
        column, plane, which, layer = chunk
        there = at + {"x": 0, "y": 0, "up": 1, "down": -1}[route]
        if there >= roles:
            there, plane = line - 1 - there, line - 1 - plane
        return group_of[there][column, plane, which, layer]

    across = {
        "x": (XSIDE, OWN, DIAG, YSIDE),
        "y": (YSIDE, DIAG, OWN, XSIDE),
        "up": (OWN, XSIDE, YSIDE, DIAG),
        "down": (OWN, XSIDE, YSIDE, DIAG),
    }

    def place(column, plane):
        return jnp.where(flip == 1, line - 1 - plane, plane) * 4 + columns[column]

    def slot(column, plane, which, layer):
        return (place(column, plane) * layer_count + layer) * 2 + which


    def own_copy(which, layer):
        src = (test_a, test_g)[which]
        return pltpu.make_async_copy(
            src.at[layer],
            buf.at[(me * layer_count + layer) * 2 + which],
            own_sem.at[0],
        )

    for which in range(2):
        for layer in range(layer_count):
            own_copy(which, layer).start()
    ids_copy = pltpu.make_async_copy(ids_hbm, ids_ref, train_sem.at[1])
    ids_copy.start()

    lower = {"x": x == 1, "y": y == 1, "up": flip == 1, "down": flip == 0}
    axis = {"x": 0, "y": 1, "up": 2, "down": 2}
    barrier = pltpu.get_barrier_semaphore()

    def greet(where, semaphore=barrier):
        pl.semaphore_signal(semaphore, inc=1, device_id=where, device_id_type=MESH)

    pl.when(x == 0)(lambda: greet({"tok": partner["x"]}))
    pl.when(y == 0)(lambda: greet({"tok": partner["y"]}))
    pl.when(has_up)(lambda: greet({"tok": me + 4}))
    for other in range(layers):
        pl.when(other > core)(functools.partial(greet, {"layer": other}))
    before = core + x + y + has_down.astype(jnp.int32)
    pl.when(before > 0)(lambda: pl.semaphore_wait(barrier, before))
    pl.when(x == 1)(lambda: greet({"tok": partner["x"]}, ready_sem.at[0]))
    pl.when(y == 1)(lambda: greet({"tok": partner["y"]}, ready_sem.at[1]))
    pl.when(has_down)(lambda: greet({"tok": me - 4}, ready_sem.at[2]))
    for other in range(layers):
        pl.when(other < core)(functools.partial(greet, {"layer": other}, ready_sem.at[3]))

    def copy(at, route, chunk, src=None):
        column, plane, which, layer = chunk
        here = slot(across[route][column], plane, which, layer)
        return pltpu.make_async_remote_copy(
            src_ref=buf.at[here] if src is None else src,
            dst_ref=buf.at[here],
            send_sem=send_sem.at[axis[route] // 2],
            recv_sem=recv_sem.at[group_there(at, route, chunk)],
            device_id={"tok": partner[route]},
            device_id_type=MESH,
        )

    def arrived(index, size):
        pltpu.make_async_remote_copy(
            src_ref=buf.at[pl.ds(0, size)],
            dst_ref=buf.at[pl.ds(0, size)],
            send_sem=send_sem.at[0],
            recv_sem=recv_sem.at[index],
            device_id={"tok": partner["x"]},
            device_id_type=MESH,
        ).wait_recv()

    steps = [plan_steps(at, layer_count, groups[at]) for at in range(roles)]
    count = len(steps[0])

    def send_own(at):
        def send(route):
            for own_route, chunk in first[at]:
                if own_route == route:
                    src = (test_a, test_g)[chunk[2]].at[chunk[3]]
                    copy(at, route, chunk, src).start()

        def answered(route):
            pl.semaphore_wait(ready_sem.at[axis[route]], 1)
            send(route)

        used = sorted({route for route, _ in first[at]}, key=routes.index)
        for route in used:
            pl.when(lower[route])(functools.partial(send, route))
        for route in used:
            pl.when(jnp.logical_not(lower[route]))(functools.partial(answered, route))

    pl.when(core > 0)(lambda: pl.delay(500))
    branch(role, 0, roles, send_own)

    for which, src in enumerate((train_a, train_g)):
        pltpu.make_async_copy(src, train.at[which], train_sem.at[0]).start()

    after = layers - 1 - core
    pl.when(after > 0)(lambda: pl.semaphore_wait(ready_sem.at[3], after))
    acc[...] = jnp.zeros_like(acc)
    _, tiles, _, tile = xbuf.shape
    labels = lax.broadcasted_iota(jnp.int32, (Q, rows), 0)
    nt = (((1,), (1,)), ((), ()))

    def exchange(step, j):
        to = lax.rem(core + step, layers)
        return pltpu.make_async_remote_copy(
            src_ref=xout.at[step - 1, j],
            dst_ref=xbuf.at[step - 1, j],
            send_sem=xs_sem.at[step - 1, j],
            recv_sem=xr_sem.at[step - 1, j],
            device_id={"layer": to},
            device_id_type=MESH,
        )

    ids_copy.wait()
    own_all = buf.at[pl.ds(me * layer_count * 2, layer_count * 2)]
    pltpu.make_async_copy(own_all, own_all, own_sem.at[0]).wait()
    pltpu.make_async_copy(train, train, train_sem.at[0]).wait()

    def relay(k, at):
        for index in steps[at][k][0]:
            group = groups[at][index]
            arrived(index, len(group))
            for _, _, out in group:
                for route, sent in out:
                    copy(at, route, sent).start()

    base = line * 4
    packed = [
        (
            ((one[1] * 4 + one[0]) * base + two[1] * 4 + two[0]) * layer_count + layer
        )
        for at in range(roles)
        for _, one, two, layer in steps[at]
    ]

    def position(code):
        plane, column = code // 4, code % 4
        plane = jnp.where(flip == 1, line - 1 - plane, plane)
        return plane * 4 + pick(column, columns)

    def step(k, carry):
        code = pick(role * count + k, packed)
        layer = code % layer_count
        one = position(code // layer_count // base)
        two = position((code // layer_count) % base)
        select = jnp.concatenate(
            [
                jnp.where(ids_ref[b] == labels, 1.0, 0.0).astype(jnp.bfloat16)
                for b in (one, two)
            ],
            axis=1,
        )

        branch(k, 0, count, lambda k0: branch(role, 0, roles, functools.partial(relay, k0)))

        def held(which):
            return jnp.concatenate(
                [buf[(b * layer_count + layer) * 2 + which] for b in (one, two)], axis=0
            )

        a_held, g_held = held(ACT), held(GRAD)

        a_gram = lax.dot_general(a_held, train[ACT, layer], nt, preferred_element_type=jnp.float32)
        g_gram = lax.dot_general(g_held, train[GRAD, layer], nt, preferred_element_type=jnp.float32)
        prod[...] = (a_gram * g_gram).astype(jnp.bfloat16)

        acc[...] += jnp.dot(select, prod[...], preferred_element_type=jnp.float32)

        @pl.when(k == count - 1)
        def _():
            for j in range(tiles):
                for step in range(1, layers):
                    theirs = lax.rem(core + step, layers) * q_block
                    xout[step - 1, j] = acc[
                        pl.ds(pl.multiple_of(theirs, q_block), q_block), pl.ds(j * tile, tile)
                    ].astype(jnp.bfloat16)
                    exchange(step, j).start()
        return carry

    lax.fori_loop(0, count, step, 0)

    def drain(at):
        sent = list(first[at])
        for group in groups[at]:
            for _, _, out in group:
                sent += out
        for i in range(2):
            total = sum(axis[route] // 2 == i for route, _ in sent)
            if total > 0:
                all_of_them = buf.at[pl.ds(0, total)]
                pltpu.make_async_remote_copy(
                    src_ref=all_of_them,
                    dst_ref=all_of_them,
                    send_sem=send_sem.at[i],
                    recv_sem=recv_sem.at[0],
                    device_id={"tok": partner["x"]},
                    device_id_type=MESH,
                ).wait_send()

    branch(role, 0, roles, drain)

    mine = pl.ds(pl.multiple_of(core * q_block, q_block), q_block)
    for j in range(tiles):
        at = pl.ds(j * tile, tile)
        for step in range(1, layers):
            exchange(step, j).wait_recv()
        result = acc[mine, at]
        for step in range(1, layers):
            result = result + xbuf[step - 1, j].astype(jnp.float32)
        out_ref[:, at] = result
    for j in range(tiles):
        for step in range(1, layers):
            exchange(step, j).wait_send()


def on_device(layers, toks, train_act, train_grad, test_act, test_grad, segment_ids):
    layer_count, train_rows, width = train_act.shape
    rows = test_act.shape[1]
    line = toks // 4
    first, log = route_blocks(line, layer_count)
    groups = [gather_groups(received) for received in log]
    tile = math.gcd(train_rows, 2048)
    tiles = train_rows // tile
    q_block = Q // layers
    ids = segment_ids.reshape(toks, 1, rows)
    dma = pltpu.SemaphoreType.DMA
    in_hbm = pl.BlockSpec(memory_space=pltpu.HBM)
    return pl.pallas_call(
        functools.partial(kernel, layers, line, first, groups),
        out_shape=pltpu.VMEM((q_block, train_rows), jnp.float32),
        in_specs=[in_hbm] * 5,
        out_specs=pl.BlockSpec(memory_space=pltpu.VMEM),
        scratch_shapes=[
            pltpu.VMEM((toks, 1, rows), jnp.int32),
            pltpu.VMEM((2 * rows, train_rows), jnp.bfloat16),
            pltpu.VMEM((2, layer_count, train_rows, width), jnp.bfloat16),
            pltpu.VMEM((toks * layer_count * 2, rows, width), jnp.bfloat16),
            pltpu.VMEM((Q, train_rows), jnp.float32),
            pltpu.VMEM((layers - 1, tiles, q_block, tile), jnp.bfloat16),
            pltpu.VMEM((layers - 1, tiles, q_block, tile), jnp.bfloat16),
            dma((2,)),
            dma((1,)),
            dma((max(len(g) for g in groups),)),
            dma((2,)),
            pltpu.SemaphoreType.REGULAR((4,)),
            dma((layers - 1, tiles)),
            dma((layers - 1, tiles)),
        ],
        compiler_params=pltpu.CompilerParams(
            collective_id=0, has_side_effects=True, vmem_limit_bytes=LIMIT
        ),
    )(train_act, train_grad, test_act, test_grad, ids)


def solution(mesh):
    placed = (
        P("layer", "tok", None),
        P("layer", "tok", None),
        P("layer", "tok", None),
        P("layer", "tok", None),
        P(),
    )
    body = functools.partial(on_device, mesh.shape["layer"], mesh.shape["tok"])
    return jax.shard_map(
        body, mesh=mesh, in_specs=placed, out_specs=P("layer", "tok"), check_vma=False
    )
```
